128 devices in a mesh: leaf: 16 (over y_hi, x, core), rep: 8 (over y_lo, z).
Axes of the slice: x: 4, y: 4 (y_hi: 2, y_lo: 2; y = y_hi * 2 + y_lo), z: 4, core: 2. Of those that a mesh axis runs over, the one named last changes fastest.
Arguments:
- local_right: float32 [16, 8, 2048, 128], P('leaf', 'rep'), may hold values from -6 to 6
- local_inverse: bfloat16 [16, 8, 16, 128, 128], P('leaf', 'rep'), may hold values from -1 to 1.4, as said below
- local_below: bfloat16 [16, 8, 15, 128, 128], P('leaf', 'rep'), may hold values from -0.5 to 0.5
- local_parent: int32 [16, 8, 15], P('leaf', 'rep'), may hold values from 1 to 15, as said below
- local_coupling: bfloat16 [16, 8, 4, 384, 2048], P('leaf', 'rep'), may hold values from -0.1 to 0.1
- separator_right: float32 [15, 384, 128], replicated, may hold values from -6 to 6
- separator_inverse: bfloat16 [15, 3, 128, 128], replicated, may hold values from -1 to 1.4, as said below
- separator_lower: bfloat16 [15, 384, 384], replicated, may hold values from -0.3125 to 0.3125
- parent_coupling: bfloat16 [14, 384, 384], replicated, may hold values from -0.3125 to 0.3125
Outputs:
- local_solution: float32 [16, 8, 2048, 128], P('leaf', 'rep')
- separator_solution: float32 [16, 4, 384, 128], P('leaf')
The draws below stay inside these ranges and needn't reach their ends.
Inputs may be any that keep to these rules, and one draw needn't show every extreme that they name: `local_parent`: entry k of a device's list is larger than k. `local_inverse`: every block is lower triangular. `separator_inverse`: every block is lower triangular.
All inputs are finite; a program needn't handle non-finite values.
Results may differ from the reference program's by a relative error of at most 0.035.
Values sent between devices are 32-bit elements; how exact they have to be, the bound alone decides.
No kernel may reach another device: no remote copies, remote signals or barrier semaphores. Data moves between devices by JAX's collectives and lax.ppermute only.
A program may use at most 128 MiB of HBM per device.

```python
import math
import jax
import jax.numpy as jnp
from jax import lax

NB = 128
R = 128
LB = 16
SB = 3
ROWS = 2048
S = 384
LEV = 4
NSEP = 15
N_LEAF = 16
N_REP = 8


def triangle_blocks(key, leading):
    first_key, second_key = jax.random.split(key)
    shape = leading + (NB, NB)
    row_index = lax.broadcasted_iota(jnp.int32, shape, len(shape) - 2)
    col_index = lax.broadcasted_iota(jnp.int32, shape, len(shape) - 1)
    diagonal = jax.random.uniform(first_key, shape, jnp.float32, 0.6, 1.4)
    offdiag = jax.random.normal(second_key, shape, jnp.float32) * (0.6 / math.sqrt(NB))
    offdiag = jnp.clip(offdiag, -0.9, 0.9)
    result = jnp.where(row_index == col_index, diagonal, jnp.where(row_index > col_index, offdiag, 0.0))
    return result.astype(jnp.bfloat16)


def draw_local_inverse(key, part):
    return triangle_blocks(key, (N_LEAF, N_REP, LB))


def draw_separator_inverse(key, part):
    return triangle_blocks(key, (NSEP, SB))


def draw_local_parent(key, part):
    shape = (N_LEAF, N_REP, LB - 1)
    index = lax.broadcasted_iota(jnp.int32, shape, 2)
    randbits = jax.random.randint(key, shape, 0, 1 << 30, dtype=jnp.int32)
    return (index + 1 + randbits % (LB - 1 - index)).astype(jnp.int32)


def draw_local_coupling(key, part):
    shape = (N_LEAF, N_REP, LEV, S, ROWS)
    height = lax.broadcasted_iota(jnp.float32, (1, 1, LEV, 1, 1), 2)
    scaling = jnp.exp2(-(height + 1.0) * 0.5) / math.sqrt(ROWS * N_REP)
    values = jnp.clip(jax.random.normal(key, shape, jnp.float32), -8.0, 8.0) * scaling
    values = jnp.clip(values, -0.09375, 0.09375)
    return values.astype(jnp.bfloat16)


def shard_levels(own_key, extent, shards, low, largest):
    def one(dim, shards_of):
        steps = jax.random.uniform(jax.random.fold_in(jax.random.fold_in(own_key, 6), dim), (shards_of,), jnp.float32, low / len(shards), largest / len(shards))
        return jnp.repeat(jnp.exp(steps), extent[dim] // shards_of).reshape((-1,) + (1,) * (len(extent) - dim - 1))

    factor_of = one(*shards[0])
    for cut in shards[1:]:
        factor_of = factor_of * one(*cut)
    return factor_of


def scatter_about(key, shape, deviation, bound, pieces=(), kind=jnp.bfloat16):
    gain = shard_levels(key, shape, pieces, -0.22, 0.18) if pieces else 1.0
    entries = jax.random.normal(key, shape, jnp.float32) * deviation * gain
    return jnp.minimum(jnp.maximum(entries, -bound), bound).astype(kind)


def setup_inputs(seed: int = 0) -> dict:
    streams_of = jax.random.split(jax.random.key(seed), 10)
    local_right = scatter_about(streams_of[0], (N_LEAF, N_REP, ROWS, R), 1.0, 6.0, ((0, 16), (1, 8)), jnp.float32)
    local_inverse = draw_local_inverse(jax.random.fold_in(streams_of[9], 71), 0)
    local_below = scatter_about(streams_of[2], (N_LEAF, N_REP, LB - 1, NB, NB), NB ** -0.5, 0.5, ((0, 16), (1, 8)))
    local_parent = draw_local_parent(jax.random.fold_in(streams_of[9], 71), 0)
    local_coupling = draw_local_coupling(jax.random.fold_in(streams_of[9], 71), 0)
    separator_right = scatter_about(streams_of[5], (NSEP, S, R), 1.0, 6.0, (), jnp.float32)
    separator_inverse = draw_separator_inverse(jax.random.fold_in(streams_of[9], 71), 0)
    separator_lower = scatter_about(streams_of[7], (NSEP, S, S), S ** -0.5, 0.3125)
    parent_coupling = scatter_about(streams_of[8], (NSEP - 1, S, S), S ** -0.5, 0.3125)
    return {"local_right": local_right, "local_inverse": local_inverse, "local_below": local_below, "local_parent": local_parent, "local_coupling": local_coupling, "separator_right": separator_right, "separator_inverse": separator_inverse, "separator_lower": separator_lower, "parent_coupling": parent_coupling}


def apply_lower(matrix, vector):
    return jnp.dot(matrix, vector.astype(jnp.bfloat16), preferred_element_type=jnp.float32)


def apply_upper(matrix, vector):
    return jnp.dot(matrix.T, vector.astype(jnp.bfloat16), preferred_element_type=jnp.float32)


def block_lookup_tables(below, parents):
    targets = jnp.concatenate([parents.astype(jnp.int32), jnp.full((1,), LB, jnp.int32)]).astype(jnp.int32)
    padded = jnp.concatenate([below, jnp.zeros((1, NB, NB), below.dtype)], axis=0)
    orders = jnp.arange(LB, dtype=jnp.int32)
    return targets, padded, orders


def local_forward(righthand, inverse, below, parents):
    columns = righthand.shape[1]
    blocks = righthand.reshape(LB, NB, columns)
    targets, padded, orders = block_lookup_tables(below, parents)

    def advance(carried, items):
        current, inv_block, low_block, target, number = items
        result = apply_lower(inv_block, current - carried[number])
        carried = carried.at[target].add(apply_lower(low_block, result))
        return carried, result

    start = jnp.zeros((LB + 1, NB, columns), jnp.float32)
    _, results = lax.scan(advance, start, (blocks, inverse, padded, targets, orders))
    return results.reshape(LB * NB, columns)


def local_backward(forward, update_terms, inverse, below, parents):
    columns = forward.shape[1]
    remains = (forward - update_terms).reshape(LB, NB, columns)
    targets, padded, orders = block_lookup_tables(below, parents)

    def retreat(carried, items):
        current, inv_block, low_block, target, number = items
        result = apply_upper(inv_block, current - apply_upper(low_block, carried[target]))
        carried = carried.at[number].set(result.astype(jnp.bfloat16))
        return carried, result

    start = jnp.zeros((LB + 1, NB, columns), jnp.bfloat16)
    _, results = lax.scan(retreat, start, (remains, inverse, padded, targets, orders), reverse=True)
    return results.reshape(LB * NB, columns)


def separator_forward(righthand, inverse, lowerpart):
    solved = []
    rounded = []
    for position in range(SB):
        current = righthand[position * NB:(position + 1) * NB]
        if position > 0:
            earlier = jnp.concatenate(rounded, axis=0)
            current = current - jnp.dot(lowerpart[position * NB:(position + 1) * NB, :position * NB], earlier, preferred_element_type=jnp.float32)
        result = apply_lower(inverse[position], current)
        solved.append(result)
        rounded.append(result.astype(jnp.bfloat16))
    return jnp.concatenate(solved, axis=0), jnp.concatenate(rounded, axis=0)


def separator_backward(righthand, inverse, lowerpart):
    solved = [None] * SB
    rounded = [None] * SB
    for position in reversed(range(SB)):
        current = righthand[position * NB:(position + 1) * NB]
        if position < SB - 1:
            later = jnp.concatenate(rounded[position + 1:], axis=0)
            current = current - apply_upper(lowerpart[(position + 1) * NB:, position * NB:(position + 1) * NB], later)
        result = apply_upper(inverse[position], current)
        solved[position] = result
        rounded[position] = result.astype(jnp.bfloat16)
    return jnp.concatenate(solved, axis=0), jnp.concatenate(rounded, axis=0)


def reference(local_right, local_inverse, local_below, local_parent, local_coupling, separator_right, separator_inverse, separator_lower, parent_coupling):
    members_all = N_LEAF * N_REP

    def flatten(array):
        return array.reshape((members_all,) + array.shape[2:])

    forward = jax.vmap(local_forward)(flatten(local_right), flatten(local_inverse), flatten(local_below), flatten(local_parent))

    def partial_sums(items):
        coupling_matrix, values = items
        rounded = values.astype(jnp.bfloat16)
        return jnp.stack([jnp.dot(coupling_matrix[height], rounded, preferred_element_type=jnp.float32) for height in range(LEV)])

    partials = lax.map(partial_sums, (flatten(local_coupling), forward))
    leaf_totals = jnp.sum(partials.reshape(N_LEAF, N_REP, LEV, S, R), axis=1)

    forward_seps = {}
    rounded_seps = {}
    for height in range(1, LEV + 1):
        groups = N_LEAF >> height
        totals = jnp.sum(leaf_totals[:, height - 1].reshape(groups, 2 ** height, S, R), axis=1)
        solved = []
        rounded = []
        for member in range(groups):
            number = groups - 1 + member
            gathered = totals[member]
            if height > 1:
                for child in (2 * member, 2 * member + 1):
                    child_number = 2 * groups - 1 + child
                    gathered = gathered + jnp.dot(parent_coupling[child_number - 1], rounded_seps[height - 1][child], preferred_element_type=jnp.float32)
            result, result_round = separator_forward(separator_right[number] - gathered, separator_inverse[number], separator_lower[number])
            solved.append(result)
            rounded.append(result_round)
        forward_seps[height] = solved
        rounded_seps[height] = rounded

    back_seps = {}
    backward_pass_rounded = {}
    for height in range(LEV, 0, -1):
        groups = N_LEAF >> height
        solved = []
        rounded = []
        for member in range(groups):
            number = groups - 1 + member
            upward = forward_seps[height][member]
            if height < LEV:
                upward = upward - apply_upper(parent_coupling[number - 1], backward_pass_rounded[height + 1][member // 2])
            result, result_round = separator_backward(upward, separator_inverse[number], separator_lower[number])
            solved.append(result)
            rounded.append(result_round)
        back_seps[height] = jnp.stack(solved)
        backward_pass_rounded[height] = rounded

    copies = [jnp.repeat(back_seps[height], 2 ** height, axis=0) for height in range(1, LEV + 1)]
    separator_solution = jnp.stack(copies, axis=1)
    rounded_all = jnp.repeat(separator_solution.astype(jnp.bfloat16), N_REP, axis=0)

    def finish(items):
        coupling_matrix, rounded, values, inverse, below, parents = items
        update_terms = jnp.dot(coupling_matrix[0].T, rounded[0], preferred_element_type=jnp.float32)
        for height in range(1, LEV):
            update_terms = update_terms + jnp.dot(coupling_matrix[height].T, rounded[height], preferred_element_type=jnp.float32)
        return local_backward(values, update_terms, inverse, below, parents)

    local_solution = lax.map(finish, (flatten(local_coupling), rounded_all, forward, flatten(local_inverse), flatten(local_below), flatten(local_parent)))
    return local_solution.reshape(N_LEAF, N_REP, ROWS, R), separator_solution
```

```python
import jax
import jax.numpy as jnp
from jax import lax
from jax.experimental import pallas as pl
from jax.experimental.pallas import tpu as pltpu
from jax.sharding import PartitionSpec as P

NB = 128
LB = 16
SB = 3
S = SB * NB
LEV = 4
CH = 8
F32 = jnp.float32
BF16 = jnp.bfloat16
VMEM = pl.BlockSpec(memory_space=pltpu.VMEM)
SMEM = pl.BlockSpec(memory_space=pltpu.SMEM)
HBM = pl.BlockSpec(memory_space=pltpu.HBM)


def limit(mib):
    return pltpu.CompilerParams(vmem_limit_bytes=mib << 20)


def mm(a, b):
    return jnp.dot(a, b, preferred_element_type=F32)


def mm_nt(a, b):
    return lax.dot_general(a, b, (((1,), (1,)), ((), ())), preferred_element_type=F32)


def first_number(height):
    return (1 << (LEV - height)) - 1


def forward_kernel(
    parent, place, right, inverse, below, coupling_hbm, sepright_hbm,
    forward_t, keep, send,
    coupling, sepright, acc, rounded, sem,
):
    leaf, rep = place[0], place[1]
    copies = [pltpu.make_async_copy(coupling_hbm, coupling, sem.at[0])]
    for h in range(1, LEV + 1):
        number = first_number(h) + (leaf >> h)
        copies.append(
            pltpu.make_async_copy(sepright_hbm.at[number], sepright.at[h - 1], sem.at[h])
        )
    for copy in copies:
        copy.start()
    acc[...] = jnp.zeros_like(acc)
    for k in range(LB):
        result = mm(inverse[k], (right[k] - acc[k]).astype(BF16))
        low = result.astype(BF16)
        rounded[k * NB : (k + 1) * NB, :] = low
        forward_t[k] = result.T
        if k < LB - 1:
            p = parent[k]
            acc[p] = acc[p] + mm(below[k], low)
    for copy in copies:
        copy.wait()
    values = rounded[...]
    first_core = lax.rem(leaf, 2) == 0
    for h in range(1, LEV + 1):
        owner = jnp.logical_and(rep == 0, lax.rem(leaf, 1 << h) == 0)
        flag = jnp.where(owner, 1.0, 0.0).astype(F32)
        for i in range(SB):
            at = (h - 1) * S + i * NB
            block = flag * sepright[h - 1, i * NB : (i + 1) * NB, :] - mm(
                coupling[at : at + NB, :], values
            )
            block = block.T
            upper, lower = block[: NB // 2], block[NB // 2 :]
            keep[:, at : at + NB] = jnp.where(first_core, upper, lower)
            send[:, at : at + NB] = jnp.where(first_core, lower, upper)


def separator_kernel(inverse, lowerpart, coupling, full, product):
    for m in range(full.shape[0]):
        i0, i1, i2 = inverse[m, 0], inverse[m, 1], inverse[m, 2]
        l10 = lowerpart[m, NB : 2 * NB, :NB]
        l20 = lowerpart[m, 2 * NB :, :NB]
        l21 = lowerpart[m, 2 * NB :, NB : 2 * NB]
        x10 = (-mm(i1, mm(l10, i0).astype(BF16))).astype(BF16)
        x21 = (-mm(i2, mm(l21, i1).astype(BF16))).astype(BF16)
        x20 = (-mm(i2, (mm(l20, i0) + mm(l21, x10)).astype(BF16))).astype(BF16)
        zero = jnp.zeros((NB, NB), BF16)
        rows = (
            jnp.concatenate([i0, zero, zero], axis=1),
            jnp.concatenate([x10, i1, zero], axis=1),
            jnp.concatenate([x20, x21, i2], axis=1),
        )
        matrix = jnp.concatenate(rows, axis=0)
        full[m] = matrix
        if m > 0:
            product[m - 1] = mm(coupling[m - 1], matrix).astype(BF16)


def subtree_kernel(parent, forward_t, inverse, below, coupling, weights, base, base_low):
    rows = 256
    total = coupling.shape[0]
    for k in reversed(range(LB)):
        inv = inverse[k]
        if k < LB - 1:
            p = parent[k]
            low = below[k]
        value = forward_t[k]
        if k < LB - 1:
            value = value - mm(base_low[p], low)
        value = mm(value.astype(BF16), inv)
        base[k] = value
        base_low[k] = value.astype(BF16)
        for at in range(0, total, rows):
            part = coupling[at : at + rows, k * NB : (k + 1) * NB]
            if k < LB - 1:
                part = (part.astype(F32) - mm(weights[p, at : at + rows, :], low)).astype(BF16)
            weights[k, at : at + rows, :] = mm(part, inv).astype(BF16)


def tree_kernel(place, gathered, full, product, out, res1, res2, res3):
    chip = place[0] >> 1
    span = [slice(h * S, (h + 1) * S) for h in range(LEV)]
    residues = []
    for g in range(8):
        r = gathered[g, :, span[0]]
        res1[g] = r
        residues.append(r.astype(BF16))
    for h in range(2, LEV + 1):
        groups = 1 << (LEV - h)
        width = 8 // groups
        children = first_number(h - 1) - 1
        following = []
        for g in range(groups):
            r = gathered[g * width, :, span[h - 1]]
            for j in range(1, width):
                r = r + gathered[g * width + j, :, span[h - 1]]
            for c in (2 * g, 2 * g + 1):
                r = r - mm_nt(residues[c], product[children + c])
            if h == 2:
                res2[g] = r
            if h == 3:
                res3[g] = r
            following.append(r if h == LEV else r.astype(BF16))
        residues = following
    own = [res1[chip], res2[chip >> 1], res3[chip >> 2], residues[0]]
    above = None
    for h in range(LEV, 0, -1):
        number = first_number(h) + (place[0] >> h)
        matrix = full[number]
        value = mm(mm_nt(own[h - 1].astype(BF16), matrix).astype(BF16), matrix)
        if h < LEV:
            value = value - mm(above, product[number - 1])
        above = value.astype(BF16)
        for j in range(out.shape[0]):
            out[j, :, span[h - 1]] = value


def finish_kernel(place, mine, other, base, weights, local, separators):
    first_core = lax.rem(place[0], 2) == 0
    a, b = mine[...], other[...]
    rows = jnp.concatenate([jnp.where(first_core, a, b), jnp.where(first_core, b, a)], axis=0)
    low = rows.astype(BF16)
    for k in range(0, LB, 2):
        pair = jnp.concatenate([weights[k], weights[k + 1]], axis=1)
        terms = mm(low, pair)
        for j in range(2):
            value = base[k + j] - terms[:, j * NB : (j + 1) * NB]
            local[(k + j) * NB : (k + j + 1) * NB, :] = value.T
    for i in range(rows.shape[1] // NB):
        separators[i * NB : (i + 1) * NB, :] = rows[:, i * NB : (i + 1) * NB].T


def shape(dims, dtype=F32):
    return jax.ShapeDtypeStruct(dims, dtype)


def on_device(
    local_right,
    local_inverse,
    local_below,
    local_parent,
    local_coupling,
    separator_right,
    separator_inverse,
    separator_lower,
    parent_coupling,
):
    rows = local_right.shape[2]
    columns = local_right.shape[3]
    half = columns // 2
    height = LEV * S
    nsep = separator_lower.shape[0]
    leaves = lax.axis_size("leaf")
    chips = [[2 * i + c for i in range(leaves // 2)] for c in range(2)]
    pairs = [(i, i ^ 1) for i in range(leaves)]
    place = jnp.stack([lax.axis_index("leaf"), lax.axis_index("rep")]).astype(jnp.int32)
    right = local_right.reshape(LB, NB, columns)
    inverse = local_inverse[0, 0]
    below = local_below[0, 0]
    parent = local_parent[0, 0]
    coupling = local_coupling.reshape(height, rows)

    forward_t, keep, send = pl.pallas_call(
        forward_kernel,
        out_shape=(shape((LB, columns, NB)), shape((half, height)), shape((half, height))),
        in_specs=[SMEM, SMEM, VMEM, VMEM, VMEM, HBM, HBM],
        out_specs=(VMEM, VMEM, VMEM),
        scratch_shapes=[
            pltpu.VMEM((height, rows), BF16),
            pltpu.VMEM((LEV, S, columns), F32),
            pltpu.VMEM((LB, NB, columns), F32),
            pltpu.VMEM((rows, columns), BF16),
            pltpu.SemaphoreType.DMA((LEV + 1,)),
        ],
        compiler_params=limit(22),
        name="forward",
    )(parent, place, right, inverse, below, coupling, separator_right)

    total = keep + lax.ppermute(send, "leaf", pairs)
    parts = lax.all_to_all(total.reshape(8, CH, height), "rep", 0, 0, tiled=True)
    sep_inverse, sep_lower, sep_coupling, _ = lax.optimization_barrier(
        (separator_inverse, separator_lower, parent_coupling, total)
    )
    full, product = pl.pallas_call(
        separator_kernel,
        out_shape=(pltpu.VMEM((nsep, S, S), BF16), pltpu.VMEM((nsep - 1, S, S), BF16)),
        in_specs=[VMEM] * 3,
        out_specs=(VMEM, VMEM),
        compiler_params=limit(22),
        cost_estimate=pl.CostEstimate(flops=6 * 10**9, transcendentals=0, bytes_accessed=2 * 10**7),
        name="separator",
    )(sep_inverse, sep_lower, sep_coupling)

    parts, full, product = lax.optimization_barrier((parts, full, product))
    summed = jnp.broadcast_to(jnp.sum(parts, axis=0, keepdims=True), (8, CH, height))
    gathered = lax.all_to_all(summed, "leaf", 0, 0, axis_index_groups=chips, tiled=True)
    forward_t, _ = lax.optimization_barrier((forward_t, summed))
    weights, base = pl.pallas_call(
        subtree_kernel,
        out_shape=(pltpu.VMEM((LB, height, NB), BF16), pltpu.VMEM((LB, columns, NB), F32)),
        in_specs=[SMEM] + [VMEM] * 4,
        out_specs=(VMEM, VMEM),
        scratch_shapes=[pltpu.VMEM((LB, columns, NB), BF16)],
        compiler_params=limit(22),
        cost_estimate=pl.CostEstimate(flops=8 * 10**9, transcendentals=0, bytes_accessed=2 * 10**7),
        name="subtree",
    )(parent, forward_t, inverse, below, coupling)

    gathered, weights, base = lax.optimization_barrier((gathered, weights, base))
    solved = pl.pallas_call(
        tree_kernel,
        out_shape=shape((8, CH, height)),
        in_specs=[SMEM] + [VMEM] * 3,
        out_specs=VMEM,
        scratch_shapes=[
            pltpu.VMEM((8, CH, S), F32),
            pltpu.VMEM((4, CH, S), F32),
            pltpu.VMEM((2, CH, S), F32),
        ],
        compiler_params=limit(16),
        name="tree",
    )(place, gathered, full, product)
    mine = lax.all_to_all(solved, "rep", 0, 0, tiled=True).reshape(half, height)
    other = lax.ppermute(mine, "leaf", pairs)
    local, separators = pl.pallas_call(
        finish_kernel,
        out_shape=(shape((rows, columns)), shape((height, columns))),
        in_specs=[SMEM] + [VMEM] * 4,
        out_specs=(VMEM, VMEM),
        compiler_params=limit(16),
        name="finish",
    )(place, mine, other, base, weights)
    return (local[None, None], separators.reshape(1, LEV, S, columns))


def solution(mesh):
    in_specs = (
        P("leaf", "rep", None, None),
        P("leaf", "rep", None, None, None),
        P("leaf", "rep", None, None, None),
        P("leaf", "rep", None),
        P("leaf", "rep", None, None, None),
        P(),
        P(),
        P(),
        P(),
    )
    out_specs = (P("leaf", "rep", None, None), P("leaf", None, None, None))
    return jax.shard_map(
        on_device, mesh=mesh, in_specs=in_specs, out_specs=out_specs, check_vma=False
    )
```

```python
import jax
import jax.numpy as jnp
from jax import lax
from jax.experimental import pallas as pl
from jax.experimental.pallas import tpu as pltpu
from jax.sharding import PartitionSpec as P

NB = 128
LB = 16
SB = 3
S = SB * NB
LEV = 4
CH = 8
F32 = jnp.float32
BF16 = jnp.bfloat16
VMEM = pl.BlockSpec(memory_space=pltpu.VMEM)
SMEM = pl.BlockSpec(memory_space=pltpu.SMEM)
HBM = pl.BlockSpec(memory_space=pltpu.HBM)


def in_hbm(*arrays):
    return [pltpu.with_memory_space_constraint(array, pltpu.HBM) for array in arrays]


def limit(mib):
    return pltpu.CompilerParams(vmem_limit_bytes=mib << 20)


def mm(a, b):
    return jnp.dot(a, b, preferred_element_type=F32)


def mm_nt(a, b):
    return lax.dot_general(a, b, (((1,), (1,)), ((), ())), preferred_element_type=F32)


def first_number(height):
    return (1 << (LEV - height)) - 1


def forward_kernel(
    place, parent_hbm, right_hbm, inverse_hbm, below_hbm, coupling_hbm, sepright_hbm,
    forward_hbm, weights_hbm, factors_hbm, keep, send,
    forward_t, weights, factors,
    parent, right, inverse, below, coupling, sepright, acc, rounded, sem, out_sem,
):
    leaf, rep = place[0], place[1]
    first = [
        pltpu.make_async_copy(parent_hbm, parent, sem.at[0]),
        pltpu.make_async_copy(inverse_hbm, inverse, sem.at[1]),
        pltpu.make_async_copy(below_hbm, below, sem.at[2]),
        pltpu.make_async_copy(right_hbm, right, sem.at[3]),
    ]
    quarters = []
    for q in range(4):
        columns = pl.ds((3 - q) * 4 * NB, 4 * NB)
        quarters.append(
            pltpu.make_async_copy(
                coupling_hbm.at[:, columns], coupling.at[:, columns], sem.at[4 + q]
            )
        )
    others = []
    for h in range(1, LEV + 1):
        number = first_number(h) + (leaf >> h)
        others.append(
            pltpu.make_async_copy(sepright_hbm.at[number], sepright.at[h - 1], sem.at[7 + h])
        )
    for copy in first + quarters + others:
        copy.start()
    acc[...] = jnp.zeros_like(acc)
    for copy in first:
        copy.wait()
    for k in range(LB):
        factors[k, :NB, :] = inverse[k]
        if k < LB - 1:
            factors[k, NB:, :] = (-mm(below[k], inverse[k])).astype(BF16)
        else:
            factors[k, NB:, :] = jnp.zeros((NB, NB), BF16)
    outward = [pltpu.make_async_copy(factors, factors_hbm, out_sem.at[LB])]
    outward[0].start()
    rows = coupling.shape[0] // 2
    for i in range(LB):
        k = i
        result = mm(inverse[k], (right[k] - acc[k]).astype(BF16))
        low = result.astype(BF16)
        rounded[k * NB : (k + 1) * NB, :] = low
        forward_t[k] = result.T
        if k < LB - 1:
            p = parent[0, 0, k]
            acc[p] = acc[p] + mm(below[k], low)
        k = LB - 1 - i
        if i % 4 == 0:
            quarters[i // 4].wait()
        own = coupling[:, k * NB : (k + 1) * NB]
        if k < LB - 1:
            p = parent[0, 0, k]
            above = [weights[p, :rows, :], weights[p, rows:, :]]
            factor = factors[k]
            for j in range(2):
                part = jnp.concatenate([own[j * rows : (j + 1) * rows], above[j]], axis=1)
                weights[k, j * rows : (j + 1) * rows, :] = mm(part, factor).astype(BF16)
        else:
            weights[k] = mm(own, inverse[k]).astype(BF16)
        outward.append(pltpu.make_async_copy(weights.at[k], weights_hbm.at[k], out_sem.at[k]))
        outward[-1].start()
    outward.append(pltpu.make_async_copy(forward_t, forward_hbm, out_sem.at[LB + 1]))
    outward[-1].start()
    for copy in others:
        copy.wait()
    values = rounded[...]
    first_core = lax.rem(leaf, 2) == 0
    for h in range(1, LEV + 1):
        owner = jnp.logical_and(rep == 0, lax.rem(leaf, 1 << h) == 0)
        flag = jnp.where(owner, 1.0, 0.0).astype(F32)
        for i in range(SB):
            at = (h - 1) * S + i * NB
            block = flag * sepright[h - 1, i * NB : (i + 1) * NB, :] - mm(
                coupling[at : at + NB, :], values
            )
            block = block.T
            upper, lower = block[: NB // 2], block[NB // 2 :]
            keep[:, at : at + NB] = jnp.where(first_core, upper, lower)
            send[:, at : at + NB] = jnp.where(first_core, lower, upper)
    for copy in outward:
        copy.wait()


def separator_kernel(
    place, inverse_hbm, lower_hbm, coupling_hbm, full_hbm, product,
    full, inverse, lowerpart, coupling, sem, out_sem,
):
    shared = first_number(1)
    number = shared + (place[0] >> 1)
    groups = []
    for at, size, source in ((shared, 1, number), (3, 4, 3), (0, 3, 0)):
        k = len(groups) * 3
        low = max(at, 1)
        count = size - (low - at)
        start = number - 1 if at == shared else low - 1
        groups.append([
            pltpu.make_async_copy(
                inverse_hbm.at[pl.ds(source, size)], inverse.at[pl.ds(at, size)], sem.at[k]
            ),
            pltpu.make_async_copy(
                lower_hbm.at[pl.ds(source, size)], lowerpart.at[pl.ds(at, size)], sem.at[k + 1]
            ),
            pltpu.make_async_copy(
                coupling_hbm.at[pl.ds(start, count)],
                coupling.at[pl.ds(low - 1, count)],
                sem.at[k + 2],
            ),
        ])
    for group in groups:
        for copy in group:
            copy.start()
    outward = []
    for group, members in zip(groups, ((shared,), range(3, shared), range(3))):
        for copy in group:
            copy.wait()
        for m in members:
            i0, i1, i2 = inverse[m, 0], inverse[m, 1], inverse[m, 2]
            l10 = lowerpart[m, NB : 2 * NB, :NB]
            l20 = lowerpart[m, 2 * NB :, :NB]
            l21 = lowerpart[m, 2 * NB :, NB : 2 * NB]
            x10 = (-mm(i1, mm(l10, i0).astype(BF16))).astype(BF16)
            x21 = (-mm(i2, mm(l21, i1).astype(BF16))).astype(BF16)
            x20 = (-mm(i2, (mm(l20, i0) + mm(l21, x10)).astype(BF16))).astype(BF16)
            zero = jnp.zeros((NB, NB), BF16)
            parts = (
                jnp.concatenate([i0, zero, zero], axis=1),
                jnp.concatenate([x10, i1, zero], axis=1),
                jnp.concatenate([x20, x21, i2], axis=1),
            )
            matrix = jnp.concatenate(parts, axis=0)
            full[m] = matrix
            outward.append(pltpu.make_async_copy(full.at[m], full_hbm.at[m], out_sem.at[m]))
            outward[-1].start()
            if m > 0:
                product[m - 1] = mm(coupling[m - 1], matrix).astype(BF16)
    for copy in outward:
        copy.wait()


def level_kernel(parts, product, out, residue):
    total = parts[0]
    for j in range(1, parts.shape[0]):
        total = total + parts[j]
    level = total[:, :S]
    residue[...] = level
    second = total[:, S : 2 * S] - mm_nt(level.astype(BF16), product[product.shape[0] - 1])
    for j in range(out.shape[0]):
        out[j, :, :S] = second
        out[j, :, S:] = total[:, 2 * S :]


def base_kernel(
    parent_hbm, forward_hbm, factors_hbm, base, parent, forward_t, factors, base_low, sem
):
    copies = [
        pltpu.make_async_copy(parent_hbm, parent, sem.at[0]),
        pltpu.make_async_copy(factors_hbm, factors, sem.at[1]),
        pltpu.make_async_copy(forward_hbm, forward_t, sem.at[2]),
    ]
    for copy in copies:
        copy.start()
    for copy in copies:
        copy.wait()
    for k in reversed(range(LB)):
        value = forward_t[k].astype(BF16)
        if k < LB - 1:
            value = jnp.concatenate([value, base_low[parent[0, 0, k]]], axis=1)
            value = mm(value, factors[k])
        else:
            value = mm(value, factors[k, :NB, :])
        base[k] = value
        base_low[k] = value.astype(BF16)


def tree_kernel(place, gathered, residue, full_hbm, product, out, res2, res3, full, sem):
    leaf = place[0]
    copies = []
    for h in range(1, LEV + 1):
        number = first_number(1) if h == 1 else first_number(h) + (leaf >> h)
        copies.append(pltpu.make_async_copy(full_hbm.at[number], full.at[h - 1], sem.at[h - 1]))
    for copy in copies:
        copy.start()
    span = [slice(h * S, (h + 1) * S) for h in range(LEV)]
    residues = []
    for h in range(2, LEV + 1):
        groups = 1 << (LEV - h)
        width = 8 // groups
        children = first_number(h - 1) - 1
        following = []
        for g in range(groups):
            r = gathered[g * width, :, span[h - 2]]
            for j in range(1, width):
                r = r + gathered[g * width + j, :, span[h - 2]]
            if h > 2:
                for c in (2 * g, 2 * g + 1):
                    r = r - mm_nt(residues[c], product[children + c])
            if h == 2:
                res2[g] = r
            if h == 3:
                res3[g] = r
            following.append(r if h == LEV else r.astype(BF16))
        residues = following
    own = [residue[...], res2[leaf >> 2], res3[leaf >> 3], residues[0]]
    above = None
    for copy in copies:
        copy.wait()
    for h in range(LEV, 0, -1):
        number = first_number(1) if h == 1 else first_number(h) + (leaf >> h)
        matrix = full[h - 1]
        value = mm(mm_nt(own[h - 1].astype(BF16), matrix).astype(BF16), matrix)
        if h < LEV:
            value = value - mm(above, product[number - 1])
        above = value.astype(BF16)
        for j in range(out.shape[0]):
            out[j, :, span[h - 1]] = value


def finish_kernel(
    place, mine, other, base, weights_hbm, local_hbm, separators_hbm,
    weights, local, separators, sem, out_sem,
):
    inward = [
        pltpu.make_async_copy(weights_hbm.at[k], weights.at[k], sem.at[k]) for k in range(LB)
    ]
    for copy in inward:
        copy.start()
    first_core = lax.rem(place[0], 2) == 0
    a, b = mine[...], other[...]
    rows = jnp.concatenate([jnp.where(first_core, a, b), jnp.where(first_core, b, a)], axis=0)
    low = rows.astype(BF16)
    for i in range(rows.shape[1] // NB):
        separators[i * NB : (i + 1) * NB, :] = rows[:, i * NB : (i + 1) * NB].T
    outward = [pltpu.make_async_copy(separators, separators_hbm, out_sem.at[0])]
    outward[0].start()
    for k in range(0, LB, 2):
        inward[k].wait()
        inward[k + 1].wait()
        terms = mm(low, jnp.concatenate([weights[k], weights[k + 1]], axis=1))
        for j in range(2):
            value = base[k + j] - terms[:, j * NB : (j + 1) * NB]
            local[(k + j) * NB : (k + j + 1) * NB, :] = value.T
        span = pl.ds(k * NB, 2 * NB)
        outward.append(
            pltpu.make_async_copy(local.at[span], local_hbm.at[span], out_sem.at[1 + k // 2])
        )
        outward[-1].start()
    for copy in outward:
        copy.wait()


def shape(dims, dtype=F32):
    return jax.ShapeDtypeStruct(dims, dtype)


def on_device(
    local_right,
    local_inverse,
    local_below,
    local_parent,
    local_coupling,
    separator_right,
    separator_inverse,
    separator_lower,
    parent_coupling,
):
    rows = local_right.shape[2]
    columns = local_right.shape[3]
    half = columns // 2
    height = LEV * S
    leaves = lax.axis_size("leaf")
    reps = lax.axis_size("rep")
    chips = [[2 * i + c for i in range(leaves // 2)] for c in range(2)]
    pairs = [(i, i ^ 1) for i in range(leaves)]
    place = jnp.stack([lax.axis_index("leaf"), lax.axis_index("rep")]).astype(jnp.int32)
    right = local_right.reshape(LB, NB, columns)
    coupling = local_coupling.reshape(height, rows)

    forward_t, weights, factors, keep, send = pl.pallas_call(
        forward_kernel,
        out_shape=(
            pltpu.HBM((LB, columns, NB), F32),
            pltpu.HBM((LB, height, NB), BF16),
            pltpu.HBM((LB, 2 * NB, NB), BF16),
            shape((half, height)),
            shape((half, height)),
        ),
        in_specs=[SMEM] + [HBM] * 6,
        out_specs=(HBM,) * 3 + (VMEM,) * 2,
        scratch_shapes=[
            pltpu.VMEM((LB, columns, NB), F32),
            pltpu.VMEM((LB, height, NB), BF16),
            pltpu.VMEM((LB, 2 * NB, NB), BF16),
            pltpu.SMEM((1, 1, LB - 1), jnp.int32),
            pltpu.VMEM((LB, NB, columns), F32),
            pltpu.VMEM((LB, NB, NB), BF16),
            pltpu.VMEM((LB - 1, NB, NB), BF16),
            pltpu.VMEM((height, rows), BF16),
            pltpu.VMEM((LEV, S, columns), F32),
            pltpu.VMEM((LB, NB, columns), F32),
            pltpu.VMEM((rows, columns), BF16),
            pltpu.SemaphoreType.DMA((12,)),
            pltpu.SemaphoreType.DMA((LB + 2,)),
        ],
        compiler_params=limit(30),
        name="forward",
    )(place, *in_hbm(local_parent, right, local_inverse[0, 0], local_below[0, 0], coupling, separator_right))

    total = keep + lax.ppermute(send, "leaf", pairs)
    parts = lax.all_to_all(total.reshape(reps, CH, height), "rep", 0, 0, tiled=True)
    place_after, _ = lax.optimization_barrier((place, total))
    full, product = pl.pallas_call(
        separator_kernel,
        out_shape=(pltpu.HBM((8, S, S), BF16), shape((7, S, S), BF16)),
        in_specs=[SMEM] + [HBM] * 3,
        out_specs=(HBM, VMEM),
        scratch_shapes=[
            pltpu.VMEM((8, S, S), BF16),
            pltpu.VMEM((8, SB, NB, NB), BF16),
            pltpu.VMEM((8, S, S), BF16),
            pltpu.VMEM((7, S, S), BF16),
            pltpu.SemaphoreType.DMA((9,)),
            pltpu.SemaphoreType.DMA((8,)),
        ],
        compiler_params=limit(16),
        cost_estimate=pl.CostEstimate(flops=6 * 10**9, transcendentals=0, bytes_accessed=2 * 10**7),
        name="separator",
    )(place_after, *in_hbm(separator_inverse, separator_lower, parent_coupling))

    parts, full, product = lax.optimization_barrier((parts, full, product))
    summed, residue = pl.pallas_call(
        level_kernel,
        out_shape=(shape((leaves // 2, CH, height - S)), shape((CH, S))),
        in_specs=[VMEM] * 2,
        out_specs=(VMEM, VMEM),
        compiler_params=limit(8),
        name="level",
    )(parts, product)
    gathered = lax.all_to_all(summed, "leaf", 0, 0, axis_index_groups=chips, tiled=True)
    forward_t, _ = lax.optimization_barrier((forward_t, residue))
    base = pl.pallas_call(
        base_kernel,
        out_shape=shape((LB, columns, NB)),
        in_specs=[HBM] * 3,
        out_specs=VMEM,
        scratch_shapes=[
            pltpu.SMEM((1, 1, LB - 1), jnp.int32),
            pltpu.VMEM((LB, columns, NB), F32),
            pltpu.VMEM((LB, 2 * NB, NB), BF16),
            pltpu.VMEM((LB, columns, NB), BF16),
            pltpu.SemaphoreType.DMA((3,)),
        ],
        compiler_params=limit(8),
        cost_estimate=pl.CostEstimate(flops=6 * 10**9, transcendentals=0, bytes_accessed=2 * 10**7),
        name="base",
    )(*in_hbm(local_parent, forward_t, factors))
    gathered, base = lax.optimization_barrier((gathered, base))

    solved = pl.pallas_call(
        tree_kernel,
        out_shape=shape((reps, CH, height)),
        in_specs=[SMEM, VMEM, VMEM, HBM, VMEM],
        out_specs=VMEM,
        scratch_shapes=[
            pltpu.VMEM((4, CH, S), F32),
            pltpu.VMEM((2, CH, S), F32),
            pltpu.VMEM((LEV, S, S), BF16),
            pltpu.SemaphoreType.DMA((LEV,)),
        ],
        compiler_params=limit(8),
        name="tree",
    )(place, gathered, residue, *in_hbm(full), product)
    mine = lax.all_to_all(solved, "rep", 0, 0, tiled=True).reshape(half, height)
    other = lax.ppermute(mine, "leaf", pairs)
    local, separators = pl.pallas_call(
        finish_kernel,
        out_shape=(pltpu.HBM((rows, columns), F32), pltpu.HBM((height, columns), F32)),
        in_specs=[SMEM] + [VMEM] * 3 + [HBM],
        out_specs=(HBM, HBM),
        scratch_shapes=[
            pltpu.VMEM((LB, height, NB), BF16),
            pltpu.VMEM((rows, columns), F32),
            pltpu.VMEM((height, columns), F32),
            pltpu.SemaphoreType.DMA((LB,)),
            pltpu.SemaphoreType.DMA((LB // 2 + 1,)),
        ],
        compiler_params=limit(16),
        name="finish",
    )(place, mine, other, base, *in_hbm(weights))
    return (local[None, None], separators.reshape(1, LEV, S, columns))


def solution(mesh):
    in_specs = (
        P("leaf", "rep", None, None),
        P("leaf", "rep", None, None, None),
        P("leaf", "rep", None, None, None),
        P("leaf", "rep", None),
        P("leaf", "rep", None, None, None),
        P(),
        P(),
        P(),
        P(),
    )
    out_specs = (P("leaf", "rep", None, None), P("leaf", None, None, None))
    return jax.shard_map(
        on_device, mesh=mesh, in_specs=in_specs, out_specs=out_specs, check_vma=False
    )
```

```python
import jax
import jax.numpy as jnp
from jax import lax
from jax.experimental import pallas as pl
from jax.experimental.pallas import tpu as pltpu
from jax.sharding import PartitionSpec as P

NB = 128
LB = 16
SB = 3
S = SB * NB
LEV = 4
CH = 8
F32 = jnp.float32
BF16 = jnp.bfloat16
VMEM = pl.BlockSpec(memory_space=pltpu.VMEM)
SMEM = pl.BlockSpec(memory_space=pltpu.SMEM)
HBM = pl.BlockSpec(memory_space=pltpu.HBM)


def in_hbm(*arrays):
    return [pltpu.with_memory_space_constraint(array, pltpu.HBM) for array in arrays]


def limit(mib):
    return pltpu.CompilerParams(vmem_limit_bytes=mib << 20)


def mm(a, b):
    return jnp.dot(a, b, preferred_element_type=F32)


def mm_nt(a, b):
    return lax.dot_general(a, b, (((1,), (1,)), ((), ())), preferred_element_type=F32)


def first_number(height):
    return (1 << (LEV - height)) - 1


def forward_kernel(
    place, parent_hbm, right_hbm, inverse_hbm, below_hbm, coupling_hbm, sepright_hbm,
    weights_hbm, base_hbm, keep, send,
    forward_t, weights, factors, base, base_low,
    parent, right, inverse, below, coupling, sepright, acc, rounded, sem, out_sem,
):
    leaf, rep = place[0], place[1]
    first = [
        pltpu.make_async_copy(parent_hbm, parent, sem.at[0]),
        pltpu.make_async_copy(inverse_hbm, inverse, sem.at[1]),
        pltpu.make_async_copy(below_hbm, below, sem.at[2]),
        pltpu.make_async_copy(right_hbm, right, sem.at[3]),
    ]
    quarters = []
    for q in range(4):
        columns = pl.ds((3 - q) * 4 * NB, 4 * NB)
        quarters.append(
            pltpu.make_async_copy(
                coupling_hbm.at[:, columns], coupling.at[:, columns], sem.at[4 + q]
            )
        )
    others = []
    for h in range(1, LEV + 1):
        number = first_number(h) + (leaf >> h)
        others.append(
            pltpu.make_async_copy(sepright_hbm.at[number], sepright.at[h - 1], sem.at[7 + h])
        )
    for copy in first + quarters + others:
        copy.start()
    acc[...] = jnp.zeros_like(acc)
    for copy in first:
        copy.wait()
    for k in range(LB):
        factors[k, :NB, :] = inverse[k]
        if k < LB - 1:
            factors[k, NB:, :] = (-mm(below[k], inverse[k])).astype(BF16)
        else:
            factors[k, NB:, :] = jnp.zeros((NB, NB), BF16)
    outward = []
    rows = coupling.shape[0] // 2
    for i in range(LB):
        k = i
        result = mm(inverse[k], (right[k] - acc[k]).astype(BF16))
        low = result.astype(BF16)
        rounded[k * NB : (k + 1) * NB, :] = low
        forward_t[k] = result.T.astype(BF16)
        if k < LB - 1:
            p = parent[0, 0, k]
            acc[p] = acc[p] + mm(below[k], low)
        k = LB - 1 - i
        if i % 4 == 0:
            quarters[i // 4].wait()
        own = coupling[:, k * NB : (k + 1) * NB]
        if k < LB - 1:
            p = parent[0, 0, k]
            above = [weights[p, :rows, :], weights[p, rows:, :]]
            factor = factors[k]
            for j in range(2):
                part = jnp.concatenate([own[j * rows : (j + 1) * rows], above[j]], axis=1)
                weights[k, j * rows : (j + 1) * rows, :] = mm(part, factor).astype(BF16)
        else:
            weights[k] = mm(own, inverse[k]).astype(BF16)
        outward.append(pltpu.make_async_copy(weights.at[k], weights_hbm.at[k], out_sem.at[k]))
        outward[-1].start()
    for copy in others:
        copy.wait()
    values = rounded[...]
    first_core = lax.rem(leaf, 2) == 0
    remaining = list(reversed(range(LB)))
    for h in range(1, LEV + 1):
        owner = jnp.logical_and(rep == 0, lax.rem(leaf, 1 << h) == 0)
        flag = jnp.where(owner, 1.0, 0.0).astype(F32)
        for i in range(SB):
            for k in remaining[:2]:
                value = forward_t[k]
                if k < LB - 1:
                    value = jnp.concatenate([value, base_low[parent[0, 0, k]]], axis=1)
                    value = mm(value, factors[k])
                else:
                    value = mm(value, inverse[k])
                base[k] = value
                base_low[k] = value.astype(BF16)
            remaining = remaining[2:]
            at = (h - 1) * S + i * NB
            block = flag * sepright[h - 1, i * NB : (i + 1) * NB, :] - mm(
                coupling[at : at + NB, :], values
            )
            block = block.T
            upper, lower = block[: NB // 2], block[NB // 2 :]
            keep[:, at : at + NB] = jnp.where(first_core, upper, lower)
            send[:, at : at + NB] = jnp.where(first_core, lower, upper)
    outward.append(pltpu.make_async_copy(base, base_hbm, out_sem.at[LB]))
    outward[-1].start()
    for copy in outward:
        copy.wait()


def separator_kernel(
    place, inverse_hbm, lower_hbm, coupling_hbm, full_hbm, product,
    full, inverse, lowerpart, coupling, sem, out_sem,
):
    shared = first_number(1)
    number = shared + (place[0] >> 1)
    groups = []
    for at, size, source in ((shared, 1, number), (3, 4, 3), (0, 3, 0)):
        k = len(groups) * 3
        low = max(at, 1)
        count = size - (low - at)
        start = number - 1 if at == shared else low - 1
        groups.append([
            pltpu.make_async_copy(
                inverse_hbm.at[pl.ds(source, size)], inverse.at[pl.ds(at, size)], sem.at[k]
            ),
            pltpu.make_async_copy(
                lower_hbm.at[pl.ds(source, size)], lowerpart.at[pl.ds(at, size)], sem.at[k + 1]
            ),
            pltpu.make_async_copy(
                coupling_hbm.at[pl.ds(start, count)],
                coupling.at[pl.ds(low - 1, count)],
                sem.at[k + 2],
            ),
        ])
    for group in groups:
        for copy in group:
            copy.start()
    outward = []
    for group, members in zip(groups, ((shared,), range(3, shared), range(3))):
        for copy in group:
            copy.wait()
        for m in members:
            i0, i1, i2 = inverse[m, 0], inverse[m, 1], inverse[m, 2]
            l10 = lowerpart[m, NB : 2 * NB, :NB]
            l20 = lowerpart[m, 2 * NB :, :NB]
            l21 = lowerpart[m, 2 * NB :, NB : 2 * NB]
            x10 = (-mm(i1, mm(l10, i0).astype(BF16))).astype(BF16)
            x21 = (-mm(i2, mm(l21, i1).astype(BF16))).astype(BF16)
            x20 = (-mm(i2, (mm(l20, i0) + mm(l21, x10)).astype(BF16))).astype(BF16)
            zero = jnp.zeros((NB, NB), BF16)
            parts = (
                jnp.concatenate([i0, zero, zero], axis=1),
                jnp.concatenate([x10, i1, zero], axis=1),
                jnp.concatenate([x20, x21, i2], axis=1),
            )
            matrix = jnp.concatenate(parts, axis=0)
            full[m] = matrix
            outward.append(pltpu.make_async_copy(full.at[m], full_hbm.at[m], out_sem.at[m]))
            outward[-1].start()
            if m > 0:
                product[m - 1] = mm(coupling[m - 1], matrix).astype(BF16)
    for copy in outward:
        copy.wait()


def level_kernel(parts, product, out, residue):
    total = parts[0]
    for j in range(1, parts.shape[0]):
        total = total + parts[j]
    level = total[:, :S]
    residue[...] = level
    second = total[:, S : 2 * S] - mm_nt(level.astype(BF16), product[product.shape[0] - 1])
    for j in range(out.shape[0]):
        out[j, :, :S] = second
        out[j, :, S:] = total[:, 2 * S :]


def tree_kernel(
    place, gathered, residue, full_hbm, product, weights_hbm, base_hbm,
    out, weights, base, res2, res3, full, sem,
):
    leaf = place[0]
    copies = []
    for h in range(1, LEV + 1):
        number = first_number(1) if h == 1 else first_number(h) + (leaf >> h)
        copies.append(pltpu.make_async_copy(full_hbm.at[number], full.at[h - 1], sem.at[h - 1]))
    fetched = [
        pltpu.make_async_copy(weights_hbm, weights, sem.at[LEV]),
        pltpu.make_async_copy(base_hbm, base, sem.at[LEV + 1]),
    ]
    for copy in copies + fetched:
        copy.start()
    span = [slice(h * S, (h + 1) * S) for h in range(LEV)]
    residues = []
    for h in range(2, LEV + 1):
        groups = 1 << (LEV - h)
        width = 8 // groups
        children = first_number(h - 1) - 1
        following = []
        for g in range(groups):
            r = gathered[g * width, :, span[h - 2]]
            for j in range(1, width):
                r = r + gathered[g * width + j, :, span[h - 2]]
            if h > 2:
                for c in (2 * g, 2 * g + 1):
                    r = r - mm_nt(residues[c], product[children + c])
            if h == 2:
                res2[g] = r
            if h == 3:
                res3[g] = r
            following.append(r if h == LEV else r.astype(BF16))
        residues = following
    own = [residue[...], res2[leaf >> 2], res3[leaf >> 3], residues[0]]
    above = None
    for copy in copies:
        copy.wait()
    for h in range(LEV, 0, -1):
        number = first_number(1) if h == 1 else first_number(h) + (leaf >> h)
        matrix = full[h - 1]
        value = mm(mm_nt(own[h - 1].astype(BF16), matrix).astype(BF16), matrix)
        if h < LEV:
            value = value - mm(above, product[number - 1])
        above = value.astype(BF16)
        for j in range(out.shape[0]):
            out[j, :, span[h - 1]] = value
    for copy in fetched:
        copy.wait()


def finish_kernel(
    place, mine, other, base, weights, local_hbm, separators_hbm, local, separators, out_sem
):
    first_core = lax.rem(place[0], 2) == 0
    a, b = mine[...], other[...]
    rows = jnp.concatenate([jnp.where(first_core, a, b), jnp.where(first_core, b, a)], axis=0)
    low = rows.astype(BF16)
    for i in range(rows.shape[1] // NB):
        separators[i * NB : (i + 1) * NB, :] = rows[:, i * NB : (i + 1) * NB].T
    outward = [pltpu.make_async_copy(separators, separators_hbm, out_sem.at[0])]
    outward[0].start()
    for k in range(0, LB, 2):
        terms = mm(low, jnp.concatenate([weights[k], weights[k + 1]], axis=1))
        for j in range(2):
            value = base[k + j] - terms[:, j * NB : (j + 1) * NB]
            local[(k + j) * NB : (k + j + 1) * NB, :] = value.T
        span = pl.ds(k * NB, 2 * NB)
        outward.append(
            pltpu.make_async_copy(local.at[span], local_hbm.at[span], out_sem.at[1 + k // 2])
        )
        outward[-1].start()
    for copy in outward:
        copy.wait()


def shape(dims, dtype=F32):
    return jax.ShapeDtypeStruct(dims, dtype)


def on_device(
    local_right,
    local_inverse,
    local_below,
    local_parent,
    local_coupling,
    separator_right,
    separator_inverse,
    separator_lower,
    parent_coupling,
):
    rows = local_right.shape[2]
    columns = local_right.shape[3]
    half = columns // 2
    height = LEV * S
    leaves = lax.axis_size("leaf")
    reps = lax.axis_size("rep")
    chips = [[2 * i + c for i in range(leaves // 2)] for c in range(2)]
    pairs = [(i, i ^ 1) for i in range(leaves)]
    place = jnp.stack([lax.axis_index("leaf"), lax.axis_index("rep")]).astype(jnp.int32)
    right = local_right.reshape(LB, NB, columns)
    coupling = local_coupling.reshape(height, rows)

    weights, base, keep, send = pl.pallas_call(
        forward_kernel,
        out_shape=(
            pltpu.HBM((LB, height, NB), BF16),
            pltpu.HBM((LB, columns, NB), F32),
            shape((half, height)),
            shape((half, height)),
        ),
        in_specs=[SMEM] + [HBM] * 6,
        out_specs=(HBM,) * 2 + (VMEM,) * 2,
        scratch_shapes=[
            pltpu.VMEM((LB, columns, NB), BF16),
            pltpu.VMEM((LB, height, NB), BF16),
            pltpu.VMEM((LB, 2 * NB, NB), BF16),
            pltpu.VMEM((LB, columns, NB), F32),
            pltpu.VMEM((LB, columns, NB), BF16),
            pltpu.SMEM((1, 1, LB - 1), jnp.int32),
            pltpu.VMEM((LB, NB, columns), F32),
            pltpu.VMEM((LB, NB, NB), BF16),
            pltpu.VMEM((LB - 1, NB, NB), BF16),
            pltpu.VMEM((height, rows), BF16),
            pltpu.VMEM((LEV, S, columns), F32),
            pltpu.VMEM((LB, NB, columns), F32),
            pltpu.VMEM((rows, columns), BF16),
            pltpu.SemaphoreType.DMA((12,)),
            pltpu.SemaphoreType.DMA((LB + 1,)),
        ],
        compiler_params=limit(30),
        name="forward",
    )(place, *in_hbm(local_parent, right, local_inverse[0, 0], local_below[0, 0], coupling, separator_right))

    total = keep + lax.ppermute(send, "leaf", pairs)
    parts = lax.all_to_all(total.reshape(reps, CH, height), "rep", 0, 0, tiled=True)
    place_after, _ = lax.optimization_barrier((place, total))
    full, product = pl.pallas_call(
        separator_kernel,
        out_shape=(pltpu.HBM((8, S, S), BF16), shape((7, S, S), BF16)),
        in_specs=[SMEM] + [HBM] * 3,
        out_specs=(HBM, VMEM),
        scratch_shapes=[
            pltpu.VMEM((8, S, S), BF16),
            pltpu.VMEM((8, SB, NB, NB), BF16),
            pltpu.VMEM((8, S, S), BF16),
            pltpu.VMEM((7, S, S), BF16),
            pltpu.SemaphoreType.DMA((9,)),
            pltpu.SemaphoreType.DMA((8,)),
        ],
        compiler_params=limit(16),
        cost_estimate=pl.CostEstimate(flops=6 * 10**9, transcendentals=0, bytes_accessed=2 * 10**7),
        name="separator",
    )(place_after, *in_hbm(separator_inverse, separator_lower, parent_coupling))

    parts, full, product = lax.optimization_barrier((parts, full, product))
    summed, residue = pl.pallas_call(
        level_kernel,
        out_shape=(shape((leaves // 2, CH, height - S)), shape((CH, S))),
        in_specs=[VMEM] * 2,
        out_specs=(VMEM, VMEM),
        compiler_params=limit(8),
        name="level",
    )(parts, product)
    gathered = lax.all_to_all(summed, "leaf", 0, 0, axis_index_groups=chips, tiled=True)
    solved, weights, base = pl.pallas_call(
        tree_kernel,
        out_shape=(
            shape((reps, CH, height)),
            pltpu.VMEM((LB, height, NB), BF16),
            pltpu.VMEM((LB, columns, NB), F32),
        ),
        in_specs=[SMEM, VMEM, VMEM, HBM, VMEM, HBM, HBM],
        out_specs=(VMEM,) * 3,
        scratch_shapes=[
            pltpu.VMEM((4, CH, S), F32),
            pltpu.VMEM((2, CH, S), F32),
            pltpu.VMEM((LEV, S, S), BF16),
            pltpu.SemaphoreType.DMA((LEV + 2,)),
        ],
        compiler_params=limit(8),
        name="tree",
    )(place, gathered, residue, *in_hbm(full), product, *in_hbm(weights, base))
    mine = lax.all_to_all(solved, "rep", 0, 0, tiled=True).reshape(half, height)
    other = lax.ppermute(mine, "leaf", pairs)
    local, separators = pl.pallas_call(
        finish_kernel,
        out_shape=(pltpu.HBM((rows, columns), F32), pltpu.HBM((height, columns), F32)),
        in_specs=[SMEM] + [VMEM] * 4,
        out_specs=(HBM, HBM),
        scratch_shapes=[
            pltpu.VMEM((rows, columns), F32),
            pltpu.VMEM((height, columns), F32),
            pltpu.SemaphoreType.DMA((LB // 2 + 1,)),
        ],
        compiler_params=limit(16),
        name="finish",
    )(place, mine, other, base, weights)
    return (local[None, None], separators.reshape(1, LEV, S, columns))


def solution(mesh):
    in_specs = (
        P("leaf", "rep", None, None),
        P("leaf", "rep", None, None, None),
        P("leaf", "rep", None, None, None),
        P("leaf", "rep", None),
        P("leaf", "rep", None, None, None),
        P(),
        P(),
        P(),
        P(),
    )
    out_specs = (P("leaf", "rep", None, None), P("leaf", None, None, None))
    return jax.shard_map(
        on_device, mesh=mesh, in_specs=in_specs, out_specs=out_specs, check_vma=False
    )
```

```python
import jax
import jax.numpy as jnp
from jax import lax
from jax.experimental import pallas as pl
from jax.experimental.pallas import tpu as pltpu
from jax.sharding import PartitionSpec as P

NB = 128
LB = 16
SB = 3
S = SB * NB
LEV = 4
CH = 8
F32 = jnp.float32
BF16 = jnp.bfloat16
VMEM = pl.BlockSpec(memory_space=pltpu.VMEM)
SMEM = pl.BlockSpec(memory_space=pltpu.SMEM)
HBM = pl.BlockSpec(memory_space=pltpu.HBM)


def in_hbm(*arrays):
    return [pltpu.with_memory_space_constraint(array, pltpu.HBM) for array in arrays]


def limit(mib):
    return pltpu.CompilerParams(vmem_limit_bytes=mib << 20)


def mm(a, b):
    return jnp.dot(a, b, preferred_element_type=F32)


def mm_nt(a, b):
    return lax.dot_general(a, b, (((1,), (1,)), ((), ())), preferred_element_type=F32)


def first_number(height):
    return (1 << (LEV - height)) - 1


def forward_kernel(
    place, parent_hbm, right_hbm, inverse_hbm, below_hbm, coupling_hbm, sepright_hbm,
    weights_hbm, forward_hbm, factors_hbm, keep, send,
    forward_t, weights_a, weights_b, factors,
    parent, right, inverse, below, coupling, sepright, acc, rounded, sem, out_sem,
):
    leaf, rep = place[0], place[1]
    first = [
        pltpu.make_async_copy(parent_hbm, parent, sem.at[0]),
        pltpu.make_async_copy(inverse_hbm, inverse, sem.at[1]),
        pltpu.make_async_copy(below_hbm, below, sem.at[2]),
        pltpu.make_async_copy(right_hbm, right, sem.at[3]),
    ]
    quarters = []
    for q in range(4):
        columns = pl.ds((3 - q) * 4 * NB, 4 * NB)
        quarters.append(
            pltpu.make_async_copy(
                coupling_hbm.at[:, columns], coupling.at[:, columns], sem.at[4 + q]
            )
        )
    others = []
    for h in range(1, LEV + 1):
        number = first_number(h) + (leaf >> h)
        others.append(
            pltpu.make_async_copy(sepright_hbm.at[number], sepright.at[h - 1], sem.at[7 + h])
        )
    for copy in first + quarters + others:
        copy.start()
    acc[...] = jnp.zeros_like(acc)
    for copy in first:
        copy.wait()

    factors[LB - 1, :NB, :] = inverse[LB - 1]
    factors[LB - 1, NB:, :] = jnp.zeros((NB, NB), BF16)

    def factor_step(k):
        factors[k, :NB, :] = inverse[k]
        factors[k, NB:, :] = (-mm(below[k], inverse[k])).astype(BF16)

    def forward_step(k):
        result = mm(inverse[k], (right[k] - acc[k]).astype(BF16))
        low = result.astype(BF16)
        rounded[k * NB : (k + 1) * NB, :] = low
        forward_t[k] = result.T.astype(BF16)
        if k < LB - 1:
            p = parent[0, 0, k]
            acc[p] = acc[p] + mm(below[k], low)

    outward = []
    rows = coupling.shape[0] // 2

    def weights_step(k, j):
        own = coupling[j * rows : (j + 1) * rows, k * NB : (k + 1) * NB]
        half = (weights_a, weights_b)[j]
        if k < LB - 1:
            part = jnp.concatenate([own, half[parent[0, 0, k]]], axis=1)
            half[k] = mm(part, factors[k]).astype(BF16)
        else:
            half[k] = mm(own, inverse[k]).astype(BF16)
        target = weights_hbm.at[k, pl.ds(j * rows, rows), :]
        outward.append(pltpu.make_async_copy(half.at[k], target, out_sem.at[2 * k + j]))
        outward[-1].start()

    for k in reversed(range(LB - 1)):
        factor_step(k)
    outward.append(pltpu.make_async_copy(factors, factors_hbm, out_sem.at[2 * LB]))
    outward[-1].start()
    for i in range(LB):
        if i % 4 == 0:
            quarters[i // 4].wait()
        weights_step(LB - 1 - i, 0)
        forward_step(i)
        weights_step(LB - 1 - i, 1)
    outward.append(pltpu.make_async_copy(forward_t, forward_hbm, out_sem.at[2 * LB + 1]))
    outward[-1].start()
    for copy in others:
        copy.wait()
    values = rounded[...]
    first_core = lax.rem(leaf, 2) == 0
    for h in range(1, LEV + 1):
        owner = jnp.logical_and(rep == 0, lax.rem(leaf, 1 << h) == 0)
        flag = jnp.where(owner, 1.0, 0.0).astype(F32)
        for i in range(SB):
            at = (h - 1) * S + i * NB
            block = flag * sepright[h - 1, i * NB : (i + 1) * NB, :] - mm(
                coupling[at : at + NB, :], values
            )
            block = block.T
            upper, lower = block[: NB // 2], block[NB // 2 :]
            keep[:, at : at + NB] = jnp.where(first_core, upper, lower)
            send[:, at : at + NB] = jnp.where(first_core, lower, upper)
    for copy in outward:
        copy.wait()


def separator_kernel(
    place, inverse_hbm, lower_hbm, coupling_hbm, full_hbm, product,
    full, inverse, lowerpart, coupling, sem, out_sem,
):
    shared = first_number(1)
    number = shared + (place[0] >> 1)
    low_rows, low_columns = pl.ds(NB, 2 * NB), pl.ds(0, 2 * NB)
    triangles, couplings = [], []
    for at, size, source in ((0, shared, 0), (shared, 1, number)):
        k = 3 * len(couplings)
        entries = pl.ds(source, size)
        triangles.append(
            pltpu.make_async_copy(inverse_hbm.at[entries], inverse.at[pl.ds(at, size)], sem.at[k])
        )
        triangles.append(
            pltpu.make_async_copy(
                lower_hbm.at[entries, low_rows, low_columns],
                lowerpart.at[pl.ds(at, size)],
                sem.at[k + 1],
            )
        )
        skip = 1 if at == 0 else 0
        couplings.append(
            pltpu.make_async_copy(
                coupling_hbm.at[pl.ds(source - 1 + skip, size - skip)],
                coupling.at[pl.ds(at - 1 + skip, size - skip)],
                sem.at[k + 2],
            )
        )
    for copy in triangles + couplings:
        copy.start()
    for copy in triangles:
        copy.wait()
    outward = []
    zero = jnp.zeros((NB, NB), BF16)
    one, two, three = slice(0, NB), slice(NB, 2 * NB), slice(2 * NB, 3 * NB)
    members = range(shared + 1)
    inv = {m: [inverse[m, i] for i in range(SB)] for m in members}
    t10 = {m: mm(lowerpart[m, one, one], inv[m][0]).astype(BF16) for m in members}
    t21 = {m: mm(lowerpart[m, two, two], inv[m][1]).astype(BF16) for m in members}
    x10 = {m: (-mm(inv[m][1], t10[m])).astype(BF16) for m in members}
    x21 = {m: (-mm(inv[m][2], t21[m])).astype(BF16) for m in members}
    t20 = {
        m: mm(lowerpart[m, two, :], jnp.concatenate([inv[m][0], x10[m]], axis=0)).astype(BF16)
        for m in members
    }
    x20 = {m: (-mm(inv[m][2], t20[m])).astype(BF16) for m in members}
    for m in members:
        full[m, one, :] = jnp.concatenate([inv[m][0], zero, zero], axis=1)
        full[m, two, :] = jnp.concatenate([x10[m], inv[m][1], zero], axis=1)
        full[m, three, :] = jnp.concatenate([x20[m], x21[m], inv[m][2]], axis=1)
        outward.append(pltpu.make_async_copy(full.at[m], full_hbm.at[m], out_sem.at[m]))
        outward[-1].start()
    for copy in couplings:
        copy.wait()
    for m in members[1:]:
        product[m - 1] = mm(coupling[m - 1], full[m]).astype(BF16)
    for copy in outward:
        copy.wait()


def level_kernel(parts, product, out, residue):
    total = parts[0]
    for j in range(1, parts.shape[0]):
        total = total + parts[j]
    level = total[:, :S]
    residue[...] = level
    second = total[:, S : 2 * S] - mm_nt(level.astype(BF16), product[product.shape[0] - 1])
    for j in range(out.shape[0]):
        out[j, :, :S] = second
        out[j, :, S:] = total[:, 2 * S :]


def tree_kernel(
    place, gathered, residue, full_hbm, product, weights_hbm, parent_hbm, forward_hbm, factors_hbm,
    out, weights, base,
    res2, res3, full, parent, forward_t, factors, base_low, sem,
):
    leaf = place[0]
    early = [
        pltpu.make_async_copy(parent_hbm, parent, sem.at[0]),
        pltpu.make_async_copy(factors_hbm, factors, sem.at[1]),
        pltpu.make_async_copy(forward_hbm, forward_t, sem.at[2]),
    ]
    for h in range(1, LEV + 1):
        number = first_number(1) if h == 1 else first_number(h) + (leaf >> h)
        early.append(pltpu.make_async_copy(full_hbm.at[number], full.at[h - 1], sem.at[2 + h]))
    fetched = pltpu.make_async_copy(weights_hbm.at[pl.ds(0, LB // 2)], weights, sem.at[3 + LEV])
    for copy in early + [fetched]:
        copy.start()
    remaining = list(reversed(range(LB)))

    def base_steps(count):
        for _ in range(min(count, len(remaining))):
            k = remaining.pop(0)
            value = forward_t[k]
            if k < LB - 1:
                value = jnp.concatenate([value, base_low[parent[0, 0, k]]], axis=1)
                value = mm(value, factors[k])
            else:
                value = mm(value, factors[k, :NB, :])
            base[k] = value
            base_low[k] = value.astype(BF16)

    span = [slice(h * S, (h + 1) * S) for h in range(LEV)]
    residues = []
    for h in range(2, LEV + 1):
        groups = 1 << (LEV - h)
        width = 8 // groups
        children = first_number(h - 1) - 1
        following = []
        for g in range(groups):
            r = gathered[g * width, :, span[h - 2]]
            for j in range(1, width):
                r = r + gathered[g * width + j, :, span[h - 2]]
            if h > 2:
                for c in (2 * g, 2 * g + 1):
                    r = r - mm_nt(residues[c], product[children + c])
                base_steps(2)
            if h == 2:
                res2[g] = r
            if h == 3:
                res3[g] = r
            following.append(r if h == LEV else r.astype(BF16))
        residues = following
        if h == 2:
            for copy in early:
                copy.wait()
    own = [residue[...], res2[leaf >> 2], res3[leaf >> 3], residues[0]]
    scaled = [None] * LEV
    for h in range(LEV, 0, -1):
        matrix = full[h - 1]
        scaled[h - 1] = mm(mm_nt(own[h - 1].astype(BF16), matrix).astype(BF16), matrix)
        base_steps(1)
    above = None
    for h in range(LEV, 0, -1):
        number = first_number(1) if h == 1 else first_number(h) + (leaf >> h)
        value = scaled[h - 1]
        if h < LEV:
            value = value - mm(above, product[number - 1])
        above = value.astype(BF16)
        base_steps(2)
        for j in range(out.shape[0]):
            out[j, :, span[h - 1]] = value
    base_steps(LB)
    fetched.wait()


def finish_kernel(
    place, mine, other, base, weights_first, weights_hbm, local_hbm, separators_hbm,
    weights_last, local, separators, sem, out_sem,
):
    inward = []
    for j in range(2):
        source = weights_hbm.at[pl.ds(LB // 2 + j * LB // 4, LB // 4)]
        target = weights_last.at[pl.ds(j * LB // 4, LB // 4)]
        inward.append(pltpu.make_async_copy(source, target, sem.at[j]))
        inward[-1].start()
    first_core = lax.rem(place[0], 2) == 0
    a, b = mine[...], other[...]
    rows = jnp.concatenate([jnp.where(first_core, a, b), jnp.where(first_core, b, a)], axis=0)
    low = rows.astype(BF16)
    for i in range(rows.shape[1] // NB):
        separators[i * NB : (i + 1) * NB, :] = rows[:, i * NB : (i + 1) * NB].T
    outward = [pltpu.make_async_copy(separators, separators_hbm, out_sem.at[0])]
    outward[0].start()
    for k in range(0, LB, 2):
        if k >= LB // 2 and k % (LB // 4) == 0:
            inward[(k - LB // 2) // (LB // 4)].wait()
        weights, at = (weights_first, k) if k < LB // 2 else (weights_last, k - LB // 2)
        terms = mm(low, jnp.concatenate([weights[at], weights[at + 1]], axis=1))
        for j in range(2):
            value = base[k + j] - terms[:, j * NB : (j + 1) * NB]
            local[(k + j) * NB : (k + j + 1) * NB, :] = value.T
        span = pl.ds(k * NB, 2 * NB)
        outward.append(
            pltpu.make_async_copy(local.at[span], local_hbm.at[span], out_sem.at[1 + k // 2])
        )
        outward[-1].start()
    for copy in outward:
        copy.wait()


def shape(dims, dtype=F32):
    return jax.ShapeDtypeStruct(dims, dtype)


def run_forward(place, parent, right, inverse, below, coupling, separator_right):
    height, rows = coupling.shape
    columns = right.shape[2]
    half = columns // 2
    return pl.pallas_call(
        forward_kernel,
        out_shape=(
            pltpu.HBM((LB, height, NB), BF16),
            pltpu.HBM((LB, columns, NB), BF16),
            pltpu.HBM((LB, 2 * NB, NB), BF16),
            shape((half, height)),
            shape((half, height)),
        ),
        in_specs=[SMEM] + [HBM] * 6,
        out_specs=(HBM,) * 3 + (VMEM,) * 2,
        scratch_shapes=[
            pltpu.VMEM((LB, columns, NB), BF16),
            pltpu.VMEM((LB, height // 2, NB), BF16),
            pltpu.VMEM((LB, height // 2, NB), BF16),
            pltpu.VMEM((LB, 2 * NB, NB), BF16),
            pltpu.SMEM((1, 1, LB - 1), jnp.int32),
            pltpu.VMEM((LB, NB, columns), F32),
            pltpu.VMEM((LB, NB, NB), BF16),
            pltpu.VMEM((LB - 1, NB, NB), BF16),
            pltpu.VMEM((height, rows), BF16),
            pltpu.VMEM((LEV, S, columns), F32),
            pltpu.VMEM((LB, NB, columns), F32),
            pltpu.VMEM((rows, columns), BF16),
            pltpu.SemaphoreType.DMA((12,)),
            pltpu.SemaphoreType.DMA((2 * LB + 2,)),
        ],
        compiler_params=limit(30),
        name="forward",
    )(place, *in_hbm(parent, right, inverse, below, coupling, separator_right))


def run_separator(place, inverse, lowerpart, coupling):
    return pl.pallas_call(
        separator_kernel,
        out_shape=(pltpu.HBM((8, S, S), BF16), shape((7, S, S), BF16)),
        in_specs=[SMEM] + [HBM] * 3,
        out_specs=(HBM, VMEM),
        scratch_shapes=[
            pltpu.VMEM((8, S, S), BF16),
            pltpu.VMEM((8, SB, NB, NB), BF16),
            pltpu.VMEM((8, 2 * NB, 2 * NB), BF16),
            pltpu.VMEM((7, S, S), BF16),
            pltpu.SemaphoreType.DMA((6,)),
            pltpu.SemaphoreType.DMA((8,)),
        ],
        compiler_params=limit(16),
        cost_estimate=pl.CostEstimate(flops=6 * 10**9, transcendentals=0, bytes_accessed=2 * 10**7),
        name="separator",
    )(place, *in_hbm(inverse, lowerpart, coupling))


def on_device(
    local_right,
    local_inverse,
    local_below,
    local_parent,
    local_coupling,
    separator_right,
    separator_inverse,
    separator_lower,
    parent_coupling,
):
    rows = local_right.shape[2]
    columns = local_right.shape[3]
    half = columns // 2
    height = LEV * S
    leaves = lax.axis_size("leaf")
    reps = lax.axis_size("rep")
    chips = [[2 * i + c for i in range(leaves // 2)] for c in range(2)]
    pairs = [(i, i ^ 1) for i in range(leaves)]
    place = jnp.stack([lax.axis_index("leaf"), lax.axis_index("rep")]).astype(jnp.int32)
    right = local_right.reshape(LB, NB, columns)
    coupling = local_coupling.reshape(height, rows)

    weights, forward_t, factors, keep, send = run_forward(
        place, local_parent, right, local_inverse[0, 0], local_below[0, 0], coupling, separator_right
    )
    total = keep + lax.ppermute(send, "leaf", pairs)
    parts = lax.all_to_all(total.reshape(reps, CH, height), "rep", 0, 0, tiled=True)
    place_after, _ = lax.optimization_barrier((place, total))
    full, product = run_separator(
        place_after, separator_inverse, separator_lower, parent_coupling
    )
    parts, full, product = lax.optimization_barrier((parts, full, product))
    summed, residue = pl.pallas_call(
        level_kernel,
        out_shape=(shape((leaves // 2, CH, height - S)), shape((CH, S))),
        in_specs=[VMEM] * 2,
        out_specs=(VMEM, VMEM),
        compiler_params=limit(8),
        name="level",
    )(parts, product)
    gathered = lax.all_to_all(summed, "leaf", 0, 0, axis_index_groups=chips, tiled=True)
    solved, weights_first, base = pl.pallas_call(
        tree_kernel,
        out_shape=(
            shape((reps, CH, height)),
            pltpu.VMEM((LB // 2, height, NB), BF16),
            pltpu.VMEM((LB, columns, NB), F32),
        ),
        in_specs=[SMEM, VMEM, VMEM, HBM, VMEM] + [HBM] * 4,
        out_specs=(VMEM,) * 3,
        scratch_shapes=[
            pltpu.VMEM((4, CH, S), F32),
            pltpu.VMEM((2, CH, S), F32),
            pltpu.VMEM((LEV, S, S), BF16),
            pltpu.SMEM((1, 1, LB - 1), jnp.int32),
            pltpu.VMEM((LB, columns, NB), BF16),
            pltpu.VMEM((LB, 2 * NB, NB), BF16),
            pltpu.VMEM((LB, columns, NB), BF16),
            pltpu.SemaphoreType.DMA((LEV + 4,)),
        ],
        compiler_params=limit(12),
        name="tree",
    )(
        place, gathered, residue, *in_hbm(full), product,
        *in_hbm(weights, local_parent, forward_t, factors),
    )
    mine = lax.all_to_all(solved, "rep", 0, 0, tiled=True).reshape(half, height)
    other = lax.ppermute(mine, "leaf", pairs)
    local, separators = pl.pallas_call(
        finish_kernel,
        out_shape=(pltpu.HBM((rows, columns), F32), pltpu.HBM((height, columns), F32)),
        in_specs=[SMEM] + [VMEM] * 4 + [HBM],
        out_specs=(HBM, HBM),
        scratch_shapes=[
            pltpu.VMEM((LB // 2, height, NB), BF16),
            pltpu.VMEM((rows, columns), F32),
            pltpu.VMEM((height, columns), F32),
            pltpu.SemaphoreType.DMA((2,)),
            pltpu.SemaphoreType.DMA((LB // 2 + 1,)),
        ],
        compiler_params=limit(16),
        name="finish",
    )(place, mine, other, base, weights_first, *in_hbm(weights))
    return (local[None, None], separators.reshape(1, LEV, S, columns))


def solution(mesh):
    in_specs = (
        P("leaf", "rep", None, None),
        P("leaf", "rep", None, None, None),
        P("leaf", "rep", None, None, None),
        P("leaf", "rep", None),
        P("leaf", "rep", None, None, None),
        P(),
        P(),
        P(),
        P(),
    )
    out_specs = (P("leaf", "rep", None, None), P("leaf", None, None, None))
    return jax.shard_map(
        on_device, mesh=mesh, in_specs=in_specs, out_specs=out_specs, check_vma=False
    )
```

```python
import jax
import jax.numpy as jnp
from jax import lax
from jax.experimental import pallas as pl
from jax.experimental.pallas import tpu as pltpu
from jax.sharding import PartitionSpec as P

NB = 128
LB = 16
SB = 3
S = SB * NB
LEV = 4
CH = 8
F32 = jnp.float32
BF16 = jnp.bfloat16
VMEM = pl.BlockSpec(memory_space=pltpu.VMEM)
SMEM = pl.BlockSpec(memory_space=pltpu.SMEM)
HBM = pl.BlockSpec(memory_space=pltpu.HBM)


def in_hbm(*arrays):
    return [pltpu.with_memory_space_constraint(array, pltpu.HBM) for array in arrays]


def limit(mib):
    return pltpu.CompilerParams(vmem_limit_bytes=mib << 20)


def mm(a, b):
    return jnp.dot(a, b, preferred_element_type=F32)


def mm_nt(a, b):
    return lax.dot_general(a, b, (((1,), (1,)), ((), ())), preferred_element_type=F32)


def first_number(height):
    return (1 << (LEV - height)) - 1


def forward_kernel(
    place, parent_hbm, right_hbm, inverse_hbm, below_hbm, coupling_hbm, sepright_hbm,
    weights_hbm, forward_hbm, factors_hbm, keep, send,
    forward_t, weights_a, weights_b, factors,
    parent, right, inverse, below, coupling, sepright, acc, rounded, sem, out_sem,
):
    leaf, rep = place[0], place[1]
    first = [
        pltpu.make_async_copy(parent_hbm, parent, sem.at[0]),
        pltpu.make_async_copy(inverse_hbm, inverse, sem.at[1]),
        pltpu.make_async_copy(below_hbm, below, sem.at[2]),
        pltpu.make_async_copy(right_hbm, right, sem.at[3]),
    ]
    quarters = []
    for q in range(4):
        columns = pl.ds((3 - q) * 4 * NB, 4 * NB)
        quarters.append(
            pltpu.make_async_copy(
                coupling_hbm.at[:, columns], coupling.at[:, columns], sem.at[4 + q]
            )
        )
    others = []
    for h in range(1, LEV + 1):
        number = first_number(h) + (leaf >> h)
        others.append(
            pltpu.make_async_copy(sepright_hbm.at[number], sepright.at[h - 1], sem.at[7 + h])
        )
    for copy in first + quarters + others:
        copy.start()
    acc[...] = jnp.zeros_like(acc)
    for copy in first:
        copy.wait()

    factors[LB - 1, :NB, :] = inverse[LB - 1]
    factors[LB - 1, NB:, :] = jnp.zeros((NB, NB), BF16)

    def factor_step(k):
        factors[k, :NB, :] = inverse[k]
        factors[k, NB:, :] = (-mm(below[k], inverse[k])).astype(BF16)

    def forward_step(k):
        result = mm(inverse[k], (right[k] - acc[k]).astype(BF16))
        low = result.astype(BF16)
        rounded[k * NB : (k + 1) * NB, :] = low
        forward_t[k] = result.T.astype(BF16)
        if k < LB - 1:
            p = parent[0, 0, k]
            acc[p] = acc[p] + mm(below[k], low)

    outward = []
    rows = coupling.shape[0] // 2

    def weights_step(k, j):
        own = coupling[j * rows : (j + 1) * rows, k * NB : (k + 1) * NB]
        half = (weights_a, weights_b)[j]
        if k < LB - 1:
            part = jnp.concatenate([own, half[parent[0, 0, k]]], axis=1)
            half[k] = mm(part, factors[k]).astype(BF16)
        else:
            half[k] = mm(own, inverse[k]).astype(BF16)
        target = weights_hbm.at[k, pl.ds(j * rows, rows), :]
        outward.append(pltpu.make_async_copy(half.at[k], target, out_sem.at[2 * k + j]))
        outward[-1].start()

    for k in reversed(range(LB - 1)):
        factor_step(k)
    outward.append(pltpu.make_async_copy(factors, factors_hbm, out_sem.at[2 * LB]))
    outward[-1].start()
    for i in range(LB):
        if i % 4 == 0:
            quarters[i // 4].wait()
        weights_step(LB - 1 - i, 0)
        forward_step(i)
        weights_step(LB - 1 - i, 1)
    outward.append(pltpu.make_async_copy(forward_t, forward_hbm, out_sem.at[2 * LB + 1]))
    outward[-1].start()
    for copy in others:
        copy.wait()
    values = rounded[...]
    first_core = lax.rem(leaf, 2) == 0
    for h in range(1, LEV + 1):
        owner = jnp.logical_and(rep == 0, lax.rem(leaf, 1 << h) == 0)
        flag = jnp.where(owner, 1.0, 0.0).astype(F32)
        for i in range(SB):
            at = (h - 1) * S + i * NB
            block = flag * sepright[h - 1, i * NB : (i + 1) * NB, :] - mm(
                coupling[at : at + NB, :], values
            )
            block = block.T
            upper, lower = block[: NB // 2], block[NB // 2 :]
            keep[:, at : at + NB] = jnp.where(first_core, upper, lower)
            send[:, at : at + NB] = jnp.where(first_core, lower, upper)
    for copy in outward:
        copy.wait()


def separator_kernel(
    place, inverse_hbm, lower_hbm, coupling_hbm, full_hbm, product,
    full, inverse, lowerpart, coupling, sem, out_sem,
):
    shared = first_number(1)
    number = shared + (place[0] >> 1)
    low_rows, low_columns = pl.ds(NB, 2 * NB), pl.ds(0, 2 * NB)
    triangles, couplings = [], []
    for at, size, source in ((0, shared, 0), (shared, 1, number)):
        k = 3 * len(couplings)
        entries = pl.ds(source, size)
        triangles.append(
            pltpu.make_async_copy(inverse_hbm.at[entries], inverse.at[pl.ds(at, size)], sem.at[k])
        )
        triangles.append(
            pltpu.make_async_copy(
                lower_hbm.at[entries, low_rows, low_columns],
                lowerpart.at[pl.ds(at, size)],
                sem.at[k + 1],
            )
        )
        skip = 1 if at == 0 else 0
        couplings.append(
            pltpu.make_async_copy(
                coupling_hbm.at[pl.ds(source - 1 + skip, size - skip)],
                coupling.at[pl.ds(at - 1 + skip, size - skip)],
                sem.at[k + 2],
            )
        )
    for copy in triangles + couplings:
        copy.start()
    for copy in triangles:
        copy.wait()
    outward = []
    zero = jnp.zeros((NB, NB), BF16)
    one, two, three = slice(0, NB), slice(NB, 2 * NB), slice(2 * NB, 3 * NB)
    members = range(shared + 1)
    inv = {m: [inverse[m, i] for i in range(SB)] for m in members}
    t10 = {m: mm(lowerpart[m, one, one], inv[m][0]).astype(BF16) for m in members}
    t21 = {m: mm(lowerpart[m, two, two], inv[m][1]).astype(BF16) for m in members}
    x10 = {m: (-mm(inv[m][1], t10[m])).astype(BF16) for m in members}
    x21 = {m: (-mm(inv[m][2], t21[m])).astype(BF16) for m in members}
    t20 = {
        m: mm(lowerpart[m, two, :], jnp.concatenate([inv[m][0], x10[m]], axis=0)).astype(BF16)
        for m in members
    }
    x20 = {m: (-mm(inv[m][2], t20[m])).astype(BF16) for m in members}
    for m in members:
        full[m, one, :] = jnp.concatenate([inv[m][0], zero, zero], axis=1)
        full[m, two, :] = jnp.concatenate([x10[m], inv[m][1], zero], axis=1)
        full[m, three, :] = jnp.concatenate([x20[m], x21[m], inv[m][2]], axis=1)
        outward.append(pltpu.make_async_copy(full.at[m], full_hbm.at[m], out_sem.at[m]))
        outward[-1].start()
    for copy in couplings:
        copy.wait()
    for m in members[1:]:
        product[m - 1] = mm(coupling[m - 1], full[m]).astype(BF16)
    for copy in outward:
        copy.wait()


def level_kernel(parts, product, out, residue):
    total = parts[0]
    for j in range(1, parts.shape[0]):
        total = total + parts[j]
    level = total[:, :S]
    residue[...] = level
    second = total[:, S : 2 * S] - mm_nt(level.astype(BF16), product[product.shape[0] - 1])
    for j in range(out.shape[0]):
        out[j, :, :S] = second
        out[j, :, S:] = total[:, 2 * S :]


def tree_kernel(
    place, gathered, residue, full_hbm, product, parent_hbm, forward_hbm, factors_hbm, out, base,
    res2, res3, full, parent, forward_t, factors, base_low, sem,
):
    leaf = place[0]
    early = [
        pltpu.make_async_copy(parent_hbm, parent, sem.at[0]),
        pltpu.make_async_copy(factors_hbm, factors, sem.at[1]),
        pltpu.make_async_copy(forward_hbm, forward_t, sem.at[2]),
    ]
    for h in range(1, LEV + 1):
        number = first_number(1) if h == 1 else first_number(h) + (leaf >> h)
        early.append(pltpu.make_async_copy(full_hbm.at[number], full.at[h - 1], sem.at[2 + h]))
    for copy in early:
        copy.start()
    remaining = list(reversed(range(LB)))

    def base_steps(count):
        for _ in range(min(count, len(remaining))):
            k = remaining.pop(0)
            value = forward_t[k]
            if k < LB - 1:
                value = jnp.concatenate([value, base_low[parent[0, 0, k]]], axis=1)
                value = mm(value, factors[k])
            else:
                value = mm(value, factors[k, :NB, :])
            base[k] = value
            base_low[k] = value.astype(BF16)

    span = [slice(h * S, (h + 1) * S) for h in range(LEV)]
    residues = []
    for h in range(2, LEV + 1):
        groups = 1 << (LEV - h)
        width = 8 // groups
        children = first_number(h - 1) - 1
        following = []
        for g in range(groups):
            r = gathered[g * width, :, span[h - 2]]
            for j in range(1, width):
                r = r + gathered[g * width + j, :, span[h - 2]]
            if h > 2:
                for c in (2 * g, 2 * g + 1):
                    r = r - mm_nt(residues[c], product[children + c])
                base_steps(2)
            if h == 2:
                res2[g] = r
            if h == 3:
                res3[g] = r
            following.append(r if h == LEV else r.astype(BF16))
        residues = following
        if h == 2:
            for copy in early:
                copy.wait()
    own = [residue[...], res2[leaf >> 2], res3[leaf >> 3], residues[0]]
    scaled = [None] * LEV
    for h in range(LEV, 0, -1):
        matrix = full[h - 1]
        scaled[h - 1] = mm(mm_nt(own[h - 1].astype(BF16), matrix).astype(BF16), matrix)
        base_steps(1)
    above = None
    for h in range(LEV, 0, -1):
        number = first_number(1) if h == 1 else first_number(h) + (leaf >> h)
        value = scaled[h - 1]
        if h < LEV:
            value = value - mm(above, product[number - 1])
        above = value.astype(BF16)
        base_steps(2)
        for j in range(out.shape[0]):
            out[j, :, span[h - 1]] = value
    base_steps(LB)


def finish_kernel(
    place, mine, other, base, weights, local_hbm, separators_hbm, local, separators, out_sem
):
    first_core = lax.rem(place[0], 2) == 0
    a, b = mine[...], other[...]
    rows = jnp.concatenate([jnp.where(first_core, a, b), jnp.where(first_core, b, a)], axis=0)
    low = rows.astype(BF16)
    for i in range(rows.shape[1] // NB):
        separators[i * NB : (i + 1) * NB, :] = rows[:, i * NB : (i + 1) * NB].T
    outward = [pltpu.make_async_copy(separators, separators_hbm, out_sem.at[0])]
    outward[0].start()
    for k in range(0, LB, 2):
        terms = mm(low, jnp.concatenate([weights[k], weights[k + 1]], axis=1))
        for j in range(2):
            value = base[k + j] - terms[:, j * NB : (j + 1) * NB]
            local[(k + j) * NB : (k + j + 1) * NB, :] = value.T
        span = pl.ds(k * NB, 2 * NB)
        outward.append(
            pltpu.make_async_copy(local.at[span], local_hbm.at[span], out_sem.at[1 + k // 2])
        )
        outward[-1].start()
    for copy in outward:
        copy.wait()


def shape(dims, dtype=F32):
    return jax.ShapeDtypeStruct(dims, dtype)


def run_forward(place, parent, right, inverse, below, coupling, separator_right):
    height, rows = coupling.shape
    columns = right.shape[2]
    half = columns // 2
    return pl.pallas_call(
        forward_kernel,
        out_shape=(
            pltpu.HBM((LB, height, NB), BF16),
            pltpu.HBM((LB, columns, NB), BF16),
            pltpu.HBM((LB, 2 * NB, NB), BF16),
            shape((half, height)),
            shape((half, height)),
        ),
        in_specs=[SMEM] + [HBM] * 6,
        out_specs=(HBM,) * 3 + (VMEM,) * 2,
        scratch_shapes=[
            pltpu.VMEM((LB, columns, NB), BF16),
            pltpu.VMEM((LB, height // 2, NB), BF16),
            pltpu.VMEM((LB, height // 2, NB), BF16),
            pltpu.VMEM((LB, 2 * NB, NB), BF16),
            pltpu.SMEM((1, 1, LB - 1), jnp.int32),
            pltpu.VMEM((LB, NB, columns), F32),
            pltpu.VMEM((LB, NB, NB), BF16),
            pltpu.VMEM((LB - 1, NB, NB), BF16),
            pltpu.VMEM((height, rows), BF16),
            pltpu.VMEM((LEV, S, columns), F32),
            pltpu.VMEM((LB, NB, columns), F32),
            pltpu.VMEM((rows, columns), BF16),
            pltpu.SemaphoreType.DMA((12,)),
            pltpu.SemaphoreType.DMA((2 * LB + 2,)),
        ],
        compiler_params=limit(30),
        name="forward",
    )(place, *in_hbm(parent, right, inverse, below, coupling, separator_right))


def run_separator(place, inverse, lowerpart, coupling):
    return pl.pallas_call(
        separator_kernel,
        out_shape=(pltpu.HBM((8, S, S), BF16), shape((7, S, S), BF16)),
        in_specs=[SMEM] + [HBM] * 3,
        out_specs=(HBM, VMEM),
        scratch_shapes=[
            pltpu.VMEM((8, S, S), BF16),
            pltpu.VMEM((8, SB, NB, NB), BF16),
            pltpu.VMEM((8, 2 * NB, 2 * NB), BF16),
            pltpu.VMEM((7, S, S), BF16),
            pltpu.SemaphoreType.DMA((6,)),
            pltpu.SemaphoreType.DMA((8,)),
        ],
        compiler_params=limit(16),
        cost_estimate=pl.CostEstimate(flops=6 * 10**9, transcendentals=0, bytes_accessed=2 * 10**7),
        name="separator",
    )(place, *in_hbm(inverse, lowerpart, coupling))


def on_device(
    local_right,
    local_inverse,
    local_below,
    local_parent,
    local_coupling,
    separator_right,
    separator_inverse,
    separator_lower,
    parent_coupling,
):
    rows = local_right.shape[2]
    columns = local_right.shape[3]
    half = columns // 2
    height = LEV * S
    leaves = lax.axis_size("leaf")
    reps = lax.axis_size("rep")
    chips = [[2 * i + c for i in range(leaves // 2)] for c in range(2)]
    pairs = [(i, i ^ 1) for i in range(leaves)]
    place = jnp.stack([lax.axis_index("leaf"), lax.axis_index("rep")]).astype(jnp.int32)
    right = local_right.reshape(LB, NB, columns)
    coupling = local_coupling.reshape(height, rows)

    weights, forward_t, factors, keep, send = run_forward(
        place, local_parent, right, local_inverse[0, 0], local_below[0, 0], coupling, separator_right
    )
    total = keep + lax.ppermute(send, "leaf", pairs)
    parts = lax.all_to_all(total.reshape(reps, CH, height), "rep", 0, 0, tiled=True)
    place_after, _ = lax.optimization_barrier((place, total))
    full, product = run_separator(
        place_after, separator_inverse, separator_lower, parent_coupling
    )
    parts, full, product = lax.optimization_barrier((parts, full, product))
    summed, residue = pl.pallas_call(
        level_kernel,
        out_shape=(shape((leaves // 2, CH, height - S)), shape((CH, S))),
        in_specs=[VMEM] * 2,
        out_specs=(VMEM, VMEM),
        compiler_params=limit(8),
        name="level",
    )(parts, product)
    gathered = lax.all_to_all(summed, "leaf", 0, 0, axis_index_groups=chips, tiled=True)
    solved, base = pl.pallas_call(
        tree_kernel,
        out_shape=(
            shape((reps, CH, height)),
            pltpu.VMEM((LB, columns, NB), F32),
        ),
        in_specs=[SMEM, VMEM, VMEM, HBM, VMEM] + [HBM] * 3,
        out_specs=(VMEM,) * 2,
        scratch_shapes=[
            pltpu.VMEM((4, CH, S), F32),
            pltpu.VMEM((2, CH, S), F32),
            pltpu.VMEM((LEV, S, S), BF16),
            pltpu.SMEM((1, 1, LB - 1), jnp.int32),
            pltpu.VMEM((LB, columns, NB), BF16),
            pltpu.VMEM((LB, 2 * NB, NB), BF16),
            pltpu.VMEM((LB, columns, NB), BF16),
            pltpu.SemaphoreType.DMA((LEV + 3,)),
        ],
        compiler_params=limit(12),
        cost_estimate=pl.CostEstimate(flops=6 * 10**9, transcendentals=0, bytes_accessed=4 * 10**7),
        name="tree",
    )(
        place, gathered, residue, *in_hbm(full), product,
        *in_hbm(local_parent, forward_t, factors),
    )
    mine = lax.all_to_all(solved, "rep", 0, 0, tiled=True).reshape(half, height)
    other = lax.ppermute(mine, "leaf", pairs)
    local, separators = pl.pallas_call(
        finish_kernel,
        out_shape=(pltpu.HBM((rows, columns), F32), pltpu.HBM((height, columns), F32)),
        in_specs=[SMEM] + [VMEM] * 4,
        out_specs=(HBM, HBM),
        scratch_shapes=[
            pltpu.VMEM((rows, columns), F32),
            pltpu.VMEM((height, columns), F32),
            pltpu.SemaphoreType.DMA((LB // 2 + 1,)),
        ],
        compiler_params=limit(16),
        name="finish",
    )(place, mine, other, base, weights)
    return (local[None, None], separators.reshape(1, LEV, S, columns))


def solution(mesh):
    in_specs = (
        P("leaf", "rep", None, None),
        P("leaf", "rep", None, None, None),
        P("leaf", "rep", None, None, None),
        P("leaf", "rep", None),
        P("leaf", "rep", None, None, None),
        P(),
        P(),
        P(),
        P(),
    )
    out_specs = (P("leaf", "rep", None, None), P("leaf", None, None, None))
    return jax.shard_map(
        on_device, mesh=mesh, in_specs=in_specs, out_specs=out_specs, check_vma=False
    )
```

```python
import jax
import jax.numpy as jnp
from jax import lax
from jax.experimental import pallas as pl
from jax.experimental.pallas import tpu as pltpu
from jax.sharding import PartitionSpec as P

NB = 128
LB = 16
SB = 3
S = SB * NB
LEV = 4
CH = 8
F32 = jnp.float32
BF16 = jnp.bfloat16
VMEM = pl.BlockSpec(memory_space=pltpu.VMEM)
SMEM = pl.BlockSpec(memory_space=pltpu.SMEM)
HBM = pl.BlockSpec(memory_space=pltpu.HBM)


def in_hbm(*arrays):
    return [pltpu.with_memory_space_constraint(array, pltpu.HBM) for array in arrays]


def limit(mib):
    return pltpu.CompilerParams(vmem_limit_bytes=mib << 20)


def mm(a, b):
    return jnp.dot(a, b, preferred_element_type=F32)


def mm_nt(a, b):
    return lax.dot_general(a, b, (((1,), (1,)), ((), ())), preferred_element_type=F32)


def first_number(height):
    return (1 << (LEV - height)) - 1


def forward_kernel(
    place, parent_hbm, right_hbm, inverse_hbm, below_hbm, coupling_hbm, sepright_hbm,
    weights_hbm, forward_t, factors, keep, send,
    weights_a, weights_b,
    parent, right, inverse, below, coupling, sepright, acc, rounded, sem, out_sem,
):
    leaf, rep = place[0], place[1]
    first = [
        pltpu.make_async_copy(parent_hbm, parent, sem.at[0]),
        pltpu.make_async_copy(inverse_hbm, inverse, sem.at[1]),
        pltpu.make_async_copy(below_hbm, below, sem.at[2]),
        pltpu.make_async_copy(right_hbm, right, sem.at[3]),
    ]
    quarters = []
    for q in range(4):
        columns = pl.ds((3 - q) * 4 * NB, 4 * NB)
        quarters.append(
            pltpu.make_async_copy(
                coupling_hbm.at[:, columns], coupling.at[:, columns], sem.at[4 + q]
            )
        )
    others = []
    for h in range(1, LEV + 1):
        number = first_number(h) + (leaf >> h)
        others.append(
            pltpu.make_async_copy(sepright_hbm.at[number], sepright.at[h - 1], sem.at[7 + h])
        )
    for copy in first + quarters + others:
        copy.start()
    acc[...] = jnp.zeros_like(acc)
    for copy in first:
        copy.wait()

    factors[LB - 1, :NB, :] = inverse[LB - 1]
    factors[LB - 1, NB:, :] = jnp.zeros((NB, NB), BF16)

    def factor_step(k):
        factors[k, :NB, :] = inverse[k]
        factors[k, NB:, :] = (-mm(below[k], inverse[k])).astype(BF16)

    def forward_step(k):
        result = mm(inverse[k], (right[k] - acc[k]).astype(BF16))
        low = result.astype(BF16)
        rounded[k * NB : (k + 1) * NB, :] = low
        forward_t[k] = result.T.astype(BF16)
        if k < LB - 1:
            p = parent[0, 0, k]
            acc[p] = acc[p] + mm(below[k], low)

    outward = []
    rows = coupling.shape[0] // 2

    def weights_step(k, j):
        own = coupling[j * rows : (j + 1) * rows, k * NB : (k + 1) * NB]
        half = (weights_a, weights_b)[j]
        if k < LB - 1:
            part = jnp.concatenate([own, half[parent[0, 0, k]]], axis=1)
            half[k] = mm(part, factors[k]).astype(BF16)
        else:
            half[k] = mm(own, inverse[k]).astype(BF16)
        target = weights_hbm.at[k, pl.ds(j * rows, rows), :]
        outward.append(pltpu.make_async_copy(half.at[k], target, out_sem.at[2 * k + j]))
        outward[-1].start()

    for k in reversed(range(LB - 1)):
        factor_step(k)
    for i in range(LB):
        if i % 4 == 0:
            quarters[i // 4].wait()
        weights_step(LB - 1 - i, 0)
        forward_step(i)
        weights_step(LB - 1 - i, 1)
    for copy in others:
        copy.wait()
    values = rounded[...]
    first_core = lax.rem(leaf, 2) == 0
    for h in range(1, LEV + 1):
        owner = jnp.logical_and(rep == 0, lax.rem(leaf, 1 << h) == 0)
        flag = jnp.where(owner, 1.0, 0.0).astype(F32)
        for i in range(SB):
            at = (h - 1) * S + i * NB
            block = flag * sepright[h - 1, i * NB : (i + 1) * NB, :] - mm(
                coupling[at : at + NB, :], values
            )
            block = block.T
            upper, lower = block[: NB // 2], block[NB // 2 :]
            keep[:, at : at + NB] = jnp.where(first_core, upper, lower)
            send[:, at : at + NB] = jnp.where(first_core, lower, upper)
    for copy in outward:
        copy.wait()


def separator_kernel(
    place, inverse_hbm, lower_hbm, coupling_hbm, parent_hbm, forward_t, factors,
    full_hbm, base_hbm, product,
    full, inverse, lowerpart, coupling, parent, base, base_low, sem, out_sem,
):
    shared = first_number(1)
    number = shared + (place[0] >> 1)
    low_rows, low_columns = pl.ds(NB, 2 * NB), pl.ds(0, 2 * NB)
    triangles, couplings = [], []
    for at, size, source in ((0, shared, 0), (shared, 1, number)):
        k = 3 * len(couplings)
        entries = pl.ds(source, size)
        triangles.append(
            pltpu.make_async_copy(inverse_hbm.at[entries], inverse.at[pl.ds(at, size)], sem.at[k])
        )
        triangles.append(
            pltpu.make_async_copy(
                lower_hbm.at[entries, low_rows, low_columns],
                lowerpart.at[pl.ds(at, size)],
                sem.at[k + 1],
            )
        )
        skip = 1 if at == 0 else 0
        couplings.append(
            pltpu.make_async_copy(
                coupling_hbm.at[pl.ds(source - 1 + skip, size - skip)],
                coupling.at[pl.ds(at - 1 + skip, size - skip)],
                sem.at[k + 2],
            )
        )
    fetched = pltpu.make_async_copy(parent_hbm, parent, sem.at[6])
    for copy in [fetched] + triangles + couplings:
        copy.start()
    remaining = list(reversed(range(LB)))

    def base_steps(count):
        for _ in range(min(count, len(remaining))):
            k = remaining.pop(0)
            value = forward_t[k]
            if k < LB - 1:
                value = jnp.concatenate([value, base_low[parent[0, 0, k]]], axis=1)
                value = mm(value, factors[k])
            else:
                value = mm(value, factors[k, :NB, :])
            base[k] = value
            base_low[k] = value.astype(BF16)

    fetched.wait()
    base_steps(3)
    for copy in triangles:
        copy.wait()
    outward = []
    zero = jnp.zeros((NB, NB), BF16)
    one, two, three = slice(0, NB), slice(NB, 2 * NB), slice(2 * NB, 3 * NB)
    members = range(shared + 1)
    inv = {m: [inverse[m, i] for i in range(SB)] for m in members}
    t10 = {m: mm(lowerpart[m, one, one], inv[m][0]).astype(BF16) for m in members}
    base_steps(1)
    t21 = {m: mm(lowerpart[m, two, two], inv[m][1]).astype(BF16) for m in members}
    base_steps(1)
    x10 = {m: (-mm(inv[m][1], t10[m])).astype(BF16) for m in members}
    base_steps(1)
    x21 = {m: (-mm(inv[m][2], t21[m])).astype(BF16) for m in members}
    base_steps(1)
    t20 = {
        m: mm(lowerpart[m, two, :], jnp.concatenate([inv[m][0], x10[m]], axis=0)).astype(BF16)
        for m in members
    }
    base_steps(1)
    x20 = {m: (-mm(inv[m][2], t20[m])).astype(BF16) for m in members}
    for m in members:
        full[m, one, :] = jnp.concatenate([inv[m][0], zero, zero], axis=1)
        full[m, two, :] = jnp.concatenate([x10[m], inv[m][1], zero], axis=1)
        full[m, three, :] = jnp.concatenate([x20[m], x21[m], inv[m][2]], axis=1)
        outward.append(pltpu.make_async_copy(full.at[m], full_hbm.at[m], out_sem.at[m]))
        outward[-1].start()
    for copy in couplings:
        copy.wait()
    for m in members[1:]:
        base_steps(2)
        product[m - 1] = mm(coupling[m - 1], full[m]).astype(BF16)
        if not remaining and len(outward) == len(members):
            outward.append(pltpu.make_async_copy(base, base_hbm, out_sem.at[len(members)]))
            outward[-1].start()
    for copy in outward:
        copy.wait()


def level_kernel(parts, product, out, residue):
    total = parts[0]
    for j in range(1, parts.shape[0]):
        total = total + parts[j]
    level = total[:, :S]
    residue[...] = level
    second = total[:, S : 2 * S] - mm_nt(level.astype(BF16), product[product.shape[0] - 1])
    for j in range(out.shape[0]):
        out[j, :, :S] = second
        out[j, :, S:] = total[:, 2 * S :]


def tree_kernel(
    place, gathered, residue, full_hbm, product, out, res2, res3, full, sem,
):
    leaf = place[0]
    early = []
    for h in range(1, LEV + 1):
        number = first_number(1) if h == 1 else first_number(h) + (leaf >> h)
        early.append(pltpu.make_async_copy(full_hbm.at[number], full.at[h - 1], sem.at[h - 1]))
    for copy in early:
        copy.start()
    span = [slice(h * S, (h + 1) * S) for h in range(LEV)]
    residues = []
    for h in range(2, LEV + 1):
        groups = 1 << (LEV - h)
        width = 8 // groups
        children = first_number(h - 1) - 1
        following = []
        for g in range(groups):
            r = gathered[g * width, :, span[h - 2]]
            for j in range(1, width):
                r = r + gathered[g * width + j, :, span[h - 2]]
            if h > 2:
                for c in (2 * g, 2 * g + 1):
                    r = r - mm_nt(residues[c], product[children + c])
            if h == 2:
                res2[g] = r
            if h == 3:
                res3[g] = r
            following.append(r if h == LEV else r.astype(BF16))
        residues = following
        if h == 2:
            for copy in early:
                copy.wait()
    own = [residue[...], res2[leaf >> 2], res3[leaf >> 3], residues[0]]
    scaled = [None] * LEV
    for h in range(LEV, 0, -1):
        matrix = full[h - 1]
        scaled[h - 1] = mm(mm_nt(own[h - 1].astype(BF16), matrix).astype(BF16), matrix)
    above = None
    for h in range(LEV, 0, -1):
        number = first_number(1) if h == 1 else first_number(h) + (leaf >> h)
        value = scaled[h - 1]
        if h < LEV:
            value = value - mm(above, product[number - 1])
        above = value.astype(BF16)
        for j in range(out.shape[0]):
            out[j, :, span[h - 1]] = value


def finish_kernel(
    place, mine, other, base, weights, local_hbm, separators_hbm, local, separators, out_sem
):
    first_core = lax.rem(place[0], 2) == 0
    a, b = mine[...], other[...]
    rows = jnp.concatenate([jnp.where(first_core, a, b), jnp.where(first_core, b, a)], axis=0)
    low = rows.astype(BF16)
    for i in range(rows.shape[1] // NB):
        separators[i * NB : (i + 1) * NB, :] = rows[:, i * NB : (i + 1) * NB].T
    outward = [pltpu.make_async_copy(separators, separators_hbm, out_sem.at[0])]
    outward[0].start()
    for k in range(0, LB, 2):
        terms = mm(low, jnp.concatenate([weights[k], weights[k + 1]], axis=1))
        for j in range(2):
            value = base[k + j] - terms[:, j * NB : (j + 1) * NB]
            local[(k + j) * NB : (k + j + 1) * NB, :] = value.T
        span = pl.ds(k * NB, 2 * NB)
        outward.append(
            pltpu.make_async_copy(local.at[span], local_hbm.at[span], out_sem.at[1 + k // 2])
        )
        outward[-1].start()
    for copy in outward:
        copy.wait()


def shape(dims, dtype=F32):
    return jax.ShapeDtypeStruct(dims, dtype)


def run_forward(place, parent, right, inverse, below, coupling, separator_right):
    height, rows = coupling.shape
    columns = right.shape[2]
    half = columns // 2
    return pl.pallas_call(
        forward_kernel,
        out_shape=(
            pltpu.HBM((LB, height, NB), BF16),
            shape((LB, columns, NB), BF16),
            shape((LB, 2 * NB, NB), BF16),
            shape((half, height)),
            shape((half, height)),
        ),
        in_specs=[SMEM] + [HBM] * 6,
        out_specs=(HBM,) + (VMEM,) * 4,
        scratch_shapes=[
            pltpu.VMEM((LB, height // 2, NB), BF16),
            pltpu.VMEM((LB, height // 2, NB), BF16),
            pltpu.SMEM((1, 1, LB - 1), jnp.int32),
            pltpu.VMEM((LB, NB, columns), F32),
            pltpu.VMEM((LB, NB, NB), BF16),
            pltpu.VMEM((LB - 1, NB, NB), BF16),
            pltpu.VMEM((height, rows), BF16),
            pltpu.VMEM((LEV, S, columns), F32),
            pltpu.VMEM((LB, NB, columns), F32),
            pltpu.VMEM((rows, columns), BF16),
            pltpu.SemaphoreType.DMA((12,)),
            pltpu.SemaphoreType.DMA((2 * LB,)),
        ],
        compiler_params=limit(30),
        name="forward",
    )(place, *in_hbm(parent, right, inverse, below, coupling, separator_right))


def run_separator(place, inverse, lowerpart, coupling, parent, forward_t, factors):
    return pl.pallas_call(
        separator_kernel,
        out_shape=(
            pltpu.HBM((8, S, S), BF16),
            pltpu.HBM(forward_t.shape, F32),
            shape((7, S, S), BF16),
        ),
        in_specs=[SMEM] + [HBM] * 4 + [VMEM] * 2,
        out_specs=(HBM, HBM, VMEM),
        scratch_shapes=[
            pltpu.VMEM((8, S, S), BF16),
            pltpu.VMEM((8, SB, NB, NB), BF16),
            pltpu.VMEM((8, 2 * NB, 2 * NB), BF16),
            pltpu.VMEM((7, S, S), BF16),
            pltpu.SMEM((1, 1, LB - 1), jnp.int32),
            pltpu.VMEM(forward_t.shape, F32),
            pltpu.VMEM(forward_t.shape, BF16),
            pltpu.SemaphoreType.DMA((7,)),
            pltpu.SemaphoreType.DMA((9,)),
        ],
        compiler_params=limit(16),
        cost_estimate=pl.CostEstimate(flops=6 * 10**9, transcendentals=0, bytes_accessed=2 * 10**7),
        name="separator",
    )(place, *in_hbm(inverse, lowerpart, coupling, parent), forward_t, factors)


def on_device(
    local_right,
    local_inverse,
    local_below,
    local_parent,
    local_coupling,
    separator_right,
    separator_inverse,
    separator_lower,
    parent_coupling,
):
    rows = local_right.shape[2]
    columns = local_right.shape[3]
    half = columns // 2
    height = LEV * S
    leaves = lax.axis_size("leaf")
    reps = lax.axis_size("rep")
    chips = [[2 * i + c for i in range(leaves // 2)] for c in range(2)]
    pairs = [(i, i ^ 1) for i in range(leaves)]
    place = jnp.stack([lax.axis_index("leaf"), lax.axis_index("rep")]).astype(jnp.int32)
    right = local_right.reshape(LB, NB, columns)
    coupling = local_coupling.reshape(height, rows)

    weights, forward_t, factors, keep, send = run_forward(
        place, local_parent, right, local_inverse[0, 0], local_below[0, 0], coupling, separator_right
    )
    total = keep + lax.ppermute(send, "leaf", pairs)
    parts = lax.all_to_all(total.reshape(reps, CH, height), "rep", 0, 0, tiled=True)
    place_after, _ = lax.optimization_barrier((place, total))
    full, base, product = run_separator(
        place_after, separator_inverse, separator_lower, parent_coupling, local_parent, forward_t, factors
    )
    parts, full, base, product = lax.optimization_barrier((parts, full, base, product))
    summed, residue = pl.pallas_call(
        level_kernel,
        out_shape=(shape((leaves // 2, CH, height - S)), shape((CH, S))),
        in_specs=[VMEM] * 2,
        out_specs=(VMEM, VMEM),
        compiler_params=limit(8),
        name="level",
    )(parts, product)
    gathered = lax.all_to_all(summed, "leaf", 0, 0, axis_index_groups=chips, tiled=True)
    solved = pl.pallas_call(
        tree_kernel,
        out_shape=shape((reps, CH, height)),
        in_specs=[SMEM, VMEM, VMEM, HBM, VMEM],
        out_specs=VMEM,
        scratch_shapes=[
            pltpu.VMEM((4, CH, S), F32),
            pltpu.VMEM((2, CH, S), F32),
            pltpu.VMEM((LEV, S, S), BF16),
            pltpu.SemaphoreType.DMA((LEV,)),
        ],
        compiler_params=limit(12),
        cost_estimate=pl.CostEstimate(flops=6 * 10**9, transcendentals=0, bytes_accessed=4 * 10**7),
        name="tree",
    )(place, gathered, residue, *in_hbm(full), product)
    mine = lax.all_to_all(solved, "rep", 0, 0, tiled=True).reshape(half, height)
    other = lax.ppermute(mine, "leaf", pairs)
    local, separators = pl.pallas_call(
        finish_kernel,
        out_shape=(pltpu.HBM((rows, columns), F32), pltpu.HBM((height, columns), F32)),
        in_specs=[SMEM] + [VMEM] * 4,
        out_specs=(HBM, HBM),
        scratch_shapes=[
            pltpu.VMEM((rows, columns), F32),
            pltpu.VMEM((height, columns), F32),
            pltpu.SemaphoreType.DMA((LB // 2 + 1,)),
        ],
        compiler_params=limit(16),
        name="finish",
    )(place, mine, other, base, weights)
    return (local[None, None], separators.reshape(1, LEV, S, columns))


def solution(mesh):
    in_specs = (
        P("leaf", "rep", None, None),
        P("leaf", "rep", None, None, None),
        P("leaf", "rep", None, None, None),
        P("leaf", "rep", None),
        P("leaf", "rep", None, None, None),
        P(),
        P(),
        P(),
        P(),
    )
    out_specs = (P("leaf", "rep", None, None), P("leaf", None, None, None))
    return jax.shard_map(
        on_device, mesh=mesh, in_specs=in_specs, out_specs=out_specs, check_vma=False
    )
```

```python
import jax
import jax.numpy as jnp
from jax import lax
from jax.experimental import pallas as pl
from jax.experimental.pallas import tpu as pltpu
from jax.sharding import PartitionSpec as P

NB = 128
LB = 16
SB = 3
S = SB * NB
LEV = 4
CH = 8
F32 = jnp.float32
BF16 = jnp.bfloat16
VMEM = pl.BlockSpec(memory_space=pltpu.VMEM)
SMEM = pl.BlockSpec(memory_space=pltpu.SMEM)
HBM = pl.BlockSpec(memory_space=pltpu.HBM)


def in_hbm(*arrays):
    return [pltpu.with_memory_space_constraint(array, pltpu.HBM) for array in arrays]


def limit(mib):
    return pltpu.CompilerParams(vmem_limit_bytes=mib << 20)


def mm(a, b):
    return jnp.dot(a, b, preferred_element_type=F32)


def mm_nt(a, b):
    return lax.dot_general(a, b, (((1,), (1,)), ((), ())), preferred_element_type=F32)


def first_number(height):
    return (1 << (LEV - height)) - 1


def forward_kernel(
    place, parent_hbm, right_hbm, inverse_hbm, below_hbm, coupling_hbm, sepright_hbm,
    weights_hbm, forward_hbm, factors_hbm, keep, send,
    forward_t, factors, weights_a, weights_b,
    parent, right, inverse, below, coupling, sepright, acc, rounded, sem, out_sem,
):
    leaf, rep = place[0], place[1]
    first = [
        pltpu.make_async_copy(parent_hbm, parent, sem.at[0]),
        pltpu.make_async_copy(inverse_hbm, inverse, sem.at[1]),
        pltpu.make_async_copy(below_hbm, below, sem.at[2]),
        pltpu.make_async_copy(right_hbm, right, sem.at[3]),
    ]
    quarters = []
    for q in range(4):
        columns = pl.ds((3 - q) * 4 * NB, 4 * NB)
        quarters.append(
            pltpu.make_async_copy(
                coupling_hbm.at[:, columns], coupling.at[:, columns], sem.at[4 + q]
            )
        )
    others = []
    for h in range(1, LEV + 1):
        number = first_number(h) + (leaf >> h)
        others.append(
            pltpu.make_async_copy(sepright_hbm.at[number], sepright.at[h - 1], sem.at[7 + h])
        )
    for copy in first + quarters + others:
        copy.start()
    acc[...] = jnp.zeros_like(acc)
    for copy in first:
        copy.wait()

    factors[LB - 1, :NB, :] = inverse[LB - 1]
    factors[LB - 1, NB:, :] = jnp.zeros((NB, NB), BF16)

    def factor_step(k):
        factors[k, :NB, :] = inverse[k]
        factors[k, NB:, :] = (-mm(below[k], inverse[k])).astype(BF16)

    def forward_step(k):
        result = mm(inverse[k], (right[k] - acc[k]).astype(BF16))
        low = result.astype(BF16)
        rounded[k * NB : (k + 1) * NB, :] = low
        forward_t[k] = result.T.astype(BF16)
        if k < LB - 1:
            p = parent[0, 0, k]
            acc[p] = acc[p] + mm(below[k], low)

    outward = []
    rows = coupling.shape[0] // 2

    def weights_step(k, j):
        own = coupling[j * rows : (j + 1) * rows, k * NB : (k + 1) * NB]
        half = (weights_a, weights_b)[j]
        if k < LB - 1:
            part = jnp.concatenate([own, half[parent[0, 0, k]]], axis=1)
            half[k] = mm(part, factors[k]).astype(BF16)
        else:
            half[k] = mm(own, inverse[k]).astype(BF16)
        target = weights_hbm.at[k, pl.ds(j * rows, rows), :]
        outward.append(pltpu.make_async_copy(half.at[k], target, out_sem.at[2 * k + j]))
        outward[-1].start()

    for k in reversed(range(LB - 1)):
        factor_step(k)
    outward.append(pltpu.make_async_copy(factors, factors_hbm, out_sem.at[2 * LB + 1]))
    outward[-1].start()
    for i in range(LB):
        if i % 4 == 0:
            quarters[i // 4].wait()
        weights_step(LB - 1 - i, 0)
        forward_step(i)
        weights_step(LB - 1 - i, 1)
    outward.append(pltpu.make_async_copy(forward_t, forward_hbm, out_sem.at[2 * LB]))
    outward[-1].start()
    for copy in others:
        copy.wait()
    values = rounded[...]
    first_core = lax.rem(leaf, 2) == 0
    for h in range(1, LEV + 1):
        owner = jnp.logical_and(rep == 0, lax.rem(leaf, 1 << h) == 0)
        flag = jnp.where(owner, 1.0, 0.0).astype(F32)
        for i in range(SB):
            at = (h - 1) * S + i * NB
            block = flag * sepright[h - 1, i * NB : (i + 1) * NB, :] - mm(
                coupling[at : at + NB, :], values
            )
            block = block.T
            upper, lower = block[: NB // 2], block[NB // 2 :]
            keep[:, at : at + NB] = jnp.where(first_core, upper, lower)
            send[:, at : at + NB] = jnp.where(first_core, lower, upper)
    for copy in outward:
        copy.wait()


def triangle(parts, zero):
    rows = (
        jnp.concatenate([parts[0], zero, zero], axis=1),
        jnp.concatenate([parts[1], parts[2], zero], axis=1),
        jnp.concatenate([parts[3], parts[4], parts[5]], axis=1),
    )
    return jnp.concatenate(rows, axis=0)


def separator_kernel(
    place, inverse_hbm, lower_hbm, coupling_hbm, parent_hbm, forward_hbm, factors_hbm,
    base_hbm, full, product,
    blocks, inverse, lowerpart, coupling, parent, forward_t, factors, base, base_low, sem,
):
    shared = first_number(1)
    number = shared + (place[0] >> 1)
    low_rows, low_columns = pl.ds(NB, 2 * NB), pl.ds(0, 2 * NB)
    triangles, couplings = [], []
    for at, size, source in ((0, shared, 0), (shared, 1, number)):
        k = 3 * len(couplings)
        entries = pl.ds(source, size)
        triangles.append(
            pltpu.make_async_copy(inverse_hbm.at[entries], inverse.at[pl.ds(at, size)], sem.at[k])
        )
        triangles.append(
            pltpu.make_async_copy(
                lower_hbm.at[entries, low_rows, low_columns],
                lowerpart.at[pl.ds(at, size)],
                sem.at[k + 1],
            )
        )
        skip = 1 if at == 0 else 0
        couplings.append(
            pltpu.make_async_copy(
                coupling_hbm.at[pl.ds(source - 1 + skip, size - skip)],
                coupling.at[pl.ds(at - 1 + skip, size - skip)],
                sem.at[k + 2],
            )
        )
    fetched = [
        pltpu.make_async_copy(parent_hbm, parent, sem.at[6]),
        pltpu.make_async_copy(forward_hbm, forward_t, sem.at[7]),
        pltpu.make_async_copy(factors_hbm, factors, sem.at[9]),
    ]
    for copy in fetched + triangles + couplings:
        copy.start()
    remaining = list(reversed(range(LB)))

    def base_steps(count):
        for _ in range(min(count, len(remaining))):
            k = remaining.pop(0)
            value = forward_t[k]
            if k < LB - 1:
                value = jnp.concatenate([value, base_low[parent[0, 0, k]]], axis=1)
                value = mm(value, factors[k])
            else:
                value = mm(value, factors[k, :NB, :])
            base[k] = value
            base_low[k] = value.astype(BF16)

    for copy in fetched:
        copy.wait()
    base_steps(3)
    for copy in triangles:
        copy.wait()
    zero = jnp.zeros((NB, NB), BF16)
    one, two, three = slice(0, NB), slice(NB, 2 * NB), slice(2 * NB, 3 * NB)
    members = range(shared + 1)
    inv = {m: [inverse[m, i] for i in range(SB)] for m in members}
    t10 = {m: mm(lowerpart[m, one, one], inv[m][0]).astype(BF16) for m in members}
    base_steps(1)
    t21 = {m: mm(lowerpart[m, two, two], inv[m][1]).astype(BF16) for m in members}
    base_steps(1)
    x10 = {m: (-mm(inv[m][1], t10[m])).astype(BF16) for m in members}
    base_steps(1)
    x21 = {m: (-mm(inv[m][2], t21[m])).astype(BF16) for m in members}
    base_steps(1)
    t20 = {
        m: mm(lowerpart[m, two, :], jnp.concatenate([inv[m][0], x10[m]], axis=0)).astype(BF16)
        for m in members
    }
    base_steps(1)
    x20 = {m: (-mm(inv[m][2], t20[m])).astype(BF16) for m in members}
    for m in members:
        for j, block in enumerate((inv[m][0], x10[m], inv[m][1], x20[m], x21[m], inv[m][2])):
            blocks[m, j] = block
    for h in range(1, LEV + 1):
        full[h - 1] = blocks[shared if h == 1 else first_number(h) + (place[0] >> h)]
    for copy in couplings:
        copy.wait()
    outward = pltpu.make_async_copy(base, base_hbm, sem.at[8])
    for m in members[1:]:
        base_steps(2)
        if m == 4:
            base_steps(LB)
            outward.start()
        matrix = triangle((inv[m][0], x10[m], inv[m][1], x20[m], x21[m], inv[m][2]), zero)
        product[m - 1] = mm(coupling[m - 1], matrix).astype(BF16)
    outward.wait()


def level_kernel(parts, product, _full, out, residue):
    total = parts[0]
    for j in range(1, parts.shape[0]):
        total = total + parts[j]
    level = total[:, :S]
    residue[...] = level
    second = total[:, S : 2 * S] - mm_nt(level.astype(BF16), product[product.shape[0] - 1])
    for j in range(out.shape[0]):
        out[j, :, :S] = second
        out[j, :, S:] = total[:, 2 * S :]


def tree_kernel(
    place, gathered, residue, full, product, out, res2, res3,
):
    leaf = place[0]
    span = [slice(h * S, (h + 1) * S) for h in range(LEV)]
    residues = []
    for h in range(2, LEV + 1):
        groups = 1 << (LEV - h)
        width = 8 // groups
        children = first_number(h - 1) - 1
        following = []
        for g in range(groups):
            r = gathered[g * width, :, span[h - 2]]
            for j in range(1, width):
                r = r + gathered[g * width + j, :, span[h - 2]]
            if h > 2:
                for c in (2 * g, 2 * g + 1):
                    r = r - mm_nt(residues[c], product[children + c])
            if h == 2:
                res2[g] = r
            if h == 3:
                res3[g] = r
            following.append(r if h == LEV else r.astype(BF16))
        residues = following
    own = [residue[...], res2[leaf >> 2], res3[leaf >> 3], residues[0]]
    scaled = [None] * LEV
    zero = jnp.zeros((NB, NB), BF16)
    for h in range(LEV, 0, -1):
        matrix = triangle([full[h - 1, j] for j in range(6)], zero)
        scaled[h - 1] = mm(mm_nt(own[h - 1].astype(BF16), matrix).astype(BF16), matrix)
    above = None
    for h in range(LEV, 0, -1):
        number = first_number(1) if h == 1 else first_number(h) + (leaf >> h)
        value = scaled[h - 1]
        if h < LEV:
            value = value - mm(above, product[number - 1])
        above = value.astype(BF16)
        for j in range(out.shape[0]):
            out[j, :, span[h - 1]] = value


def finish_kernel(
    place, mine, other, base, weights, local_hbm, separators_hbm, local, separators, out_sem
):
    first_core = lax.rem(place[0], 2) == 0
    a, b = mine[...], other[...]
    rows = jnp.concatenate([jnp.where(first_core, a, b), jnp.where(first_core, b, a)], axis=0)
    low = rows.astype(BF16)
    for i in range(rows.shape[1] // NB):
        separators[i * NB : (i + 1) * NB, :] = rows[:, i * NB : (i + 1) * NB].T
    outward = [pltpu.make_async_copy(separators, separators_hbm, out_sem.at[0])]
    outward[0].start()
    for k in range(0, LB, 2):
        terms = mm(low, jnp.concatenate([weights[k], weights[k + 1]], axis=1))
        for j in range(2):
            value = base[k + j] - terms[:, j * NB : (j + 1) * NB]
            local[(k + j) * NB : (k + j + 1) * NB, :] = value.T
        span = pl.ds(k * NB, 2 * NB)
        outward.append(
            pltpu.make_async_copy(local.at[span], local_hbm.at[span], out_sem.at[1 + k // 2])
        )
        outward[-1].start()
    for copy in outward:
        copy.wait()


def shape(dims, dtype=F32):
    return jax.ShapeDtypeStruct(dims, dtype)


def run_forward(place, parent, right, inverse, below, coupling, separator_right):
    height, rows = coupling.shape
    columns = right.shape[2]
    half = columns // 2
    return pl.pallas_call(
        forward_kernel,
        out_shape=(
            pltpu.HBM((LB, height, NB), BF16),
            pltpu.HBM((LB, columns, NB), BF16),
            pltpu.HBM((LB, 2 * NB, NB), BF16),
            shape((half, height)),
            shape((half, height)),
        ),
        in_specs=[SMEM] + [HBM] * 6,
        out_specs=(HBM,) * 3 + (VMEM,) * 2,
        scratch_shapes=[
            pltpu.VMEM((LB, columns, NB), BF16),
            pltpu.VMEM((LB, 2 * NB, NB), BF16),
            pltpu.VMEM((LB, height // 2, NB), BF16),
            pltpu.VMEM((LB, height // 2, NB), BF16),
            pltpu.SMEM((1, 1, LB - 1), jnp.int32),
            pltpu.VMEM((LB, NB, columns), F32),
            pltpu.VMEM((LB, NB, NB), BF16),
            pltpu.VMEM((LB - 1, NB, NB), BF16),
            pltpu.VMEM((height, rows), BF16),
            pltpu.VMEM((LEV, S, columns), F32),
            pltpu.VMEM((LB, NB, columns), F32),
            pltpu.VMEM((rows, columns), BF16),
            pltpu.SemaphoreType.DMA((12,)),
            pltpu.SemaphoreType.DMA((2 * LB + 2,)),
        ],
        compiler_params=limit(30),
        name="forward",
    )(place, *in_hbm(parent, right, inverse, below, coupling, separator_right))


def run_separator(place, inverse, lowerpart, coupling, parent, forward_t, factors):
    return pl.pallas_call(
        separator_kernel,
        out_shape=(
            pltpu.HBM(forward_t.shape, F32),
            shape((LEV, 6, NB, NB), BF16),
            shape((7, S, S), BF16),
        ),
        in_specs=[SMEM] + [HBM] * 6,
        out_specs=(HBM, VMEM, VMEM),
        scratch_shapes=[
            pltpu.VMEM((8, 6, NB, NB), BF16),
            pltpu.VMEM((8, SB, NB, NB), BF16),
            pltpu.VMEM((8, 2 * NB, 2 * NB), BF16),
            pltpu.VMEM((7, S, S), BF16),
            pltpu.SMEM((1, 1, LB - 1), jnp.int32),
            pltpu.VMEM(forward_t.shape, BF16),
            pltpu.VMEM(factors.shape, BF16),
            pltpu.VMEM(forward_t.shape, F32),
            pltpu.VMEM(forward_t.shape, BF16),
            pltpu.SemaphoreType.DMA((10,)),
        ],
        compiler_params=limit(16),
        cost_estimate=pl.CostEstimate(flops=6 * 10**9, transcendentals=0, bytes_accessed=2 * 10**7),
        name="separator",
    )(place, *in_hbm(inverse, lowerpart, coupling, parent, forward_t, factors))


def on_device(
    local_right,
    local_inverse,
    local_below,
    local_parent,
    local_coupling,
    separator_right,
    separator_inverse,
    separator_lower,
    parent_coupling,
):
    rows = local_right.shape[2]
    columns = local_right.shape[3]
    half = columns // 2
    height = LEV * S
    leaves = lax.axis_size("leaf")
    reps = lax.axis_size("rep")
    chips = [[2 * i + c for i in range(leaves // 2)] for c in range(2)]
    pairs = [(i, i ^ 1) for i in range(leaves)]
    place = jnp.stack([lax.axis_index("leaf"), lax.axis_index("rep")]).astype(jnp.int32)
    right = local_right.reshape(LB, NB, columns)
    coupling = local_coupling.reshape(height, rows)

    weights, forward_t, factors, keep, send = run_forward(
        place, local_parent, right, local_inverse[0, 0], local_below[0, 0], coupling, separator_right
    )
    total = keep + lax.ppermute(send, "leaf", pairs)
    parts = lax.all_to_all(total.reshape(reps, CH, height), "rep", 0, 0, tiled=True)
    place_after, _ = lax.optimization_barrier((place, total))
    base, full, product = run_separator(
        place_after, separator_inverse, separator_lower, parent_coupling, local_parent, forward_t, factors
    )
    parts, full, base, product = lax.optimization_barrier((parts, full, base, product))
    summed, residue = pl.pallas_call(
        level_kernel,
        out_shape=(shape((leaves // 2, CH, height - S)), shape((CH, S))),
        in_specs=[VMEM] * 2 + [pl.BlockSpec(memory_space=pl.ANY)],
        out_specs=(VMEM, VMEM),
        compiler_params=limit(8),
        name="level",
    )(parts, product, full)
    gathered = lax.all_to_all(summed, "leaf", 0, 0, axis_index_groups=chips, tiled=True)
    solved = pl.pallas_call(
        tree_kernel,
        out_shape=shape((reps, CH, height)),
        in_specs=[SMEM] + [VMEM] * 4,
        out_specs=VMEM,
        scratch_shapes=[
            pltpu.VMEM((4, CH, S), F32),
            pltpu.VMEM((2, CH, S), F32),
        ],
        compiler_params=limit(12),
        cost_estimate=pl.CostEstimate(flops=6 * 10**9, transcendentals=0, bytes_accessed=4 * 10**7),
        name="tree",
    )(place, gathered, residue, full, product)
    mine = lax.all_to_all(solved, "rep", 0, 0, tiled=True).reshape(half, height)
    other = lax.ppermute(mine, "leaf", pairs)
    local, separators = pl.pallas_call(
        finish_kernel,
        out_shape=(pltpu.HBM((rows, columns), F32), pltpu.HBM((height, columns), F32)),
        in_specs=[SMEM] + [VMEM] * 4,
        out_specs=(HBM, HBM),
        scratch_shapes=[
            pltpu.VMEM((rows, columns), F32),
            pltpu.VMEM((height, columns), F32),
            pltpu.SemaphoreType.DMA((LB // 2 + 1,)),
        ],
        compiler_params=limit(16),
        name="finish",
    )(place, mine, other, base, weights)
    return (local[None, None], separators.reshape(1, LEV, S, columns))


def solution(mesh):
    in_specs = (
        P("leaf", "rep", None, None),
        P("leaf", "rep", None, None, None),
        P("leaf", "rep", None, None, None),
        P("leaf", "rep", None),
        P("leaf", "rep", None, None, None),
        P(),
        P(),
        P(),
        P(),
    )
    out_specs = (P("leaf", "rep", None, None), P("leaf", None, None, None))
    return jax.shard_map(
        on_device, mesh=mesh, in_specs=in_specs, out_specs=out_specs, check_vma=False
    )
```

```python
import jax
import jax.numpy as jnp
from jax import lax
from jax.experimental import pallas as pl
from jax.experimental.pallas import tpu as pltpu
from jax.sharding import PartitionSpec as P

NB = 128
LB = 16
SB = 3
S = SB * NB
LEV = 4
CH = 8
F32 = jnp.float32
BF16 = jnp.bfloat16
VMEM = pl.BlockSpec(memory_space=pltpu.VMEM)
SMEM = pl.BlockSpec(memory_space=pltpu.SMEM)
HBM = pl.BlockSpec(memory_space=pltpu.HBM)


def in_hbm(*arrays):
    return [pltpu.with_memory_space_constraint(array, pltpu.HBM) for array in arrays]


def limit(mib):
    return pltpu.CompilerParams(vmem_limit_bytes=mib << 20)


def mm(a, b):
    return jnp.dot(a, b, preferred_element_type=F32)


def mm_nt(a, b):
    return lax.dot_general(a, b, (((1,), (1,)), ((), ())), preferred_element_type=F32)


def first_number(height):
    return (1 << (LEV - height)) - 1


def forward_kernel(
    place, parent_hbm, right_hbm, inverse_hbm, below_hbm, coupling_hbm, sepright_hbm,
    weights_hbm, forward_hbm, factors_hbm, keep, send,
    forward_t, factors, weights_a, weights_b,
    parent, right, inverse, below, coupling, sepright, acc, rounded, sem, out_sem,
):
    leaf, rep = place[0], place[1]
    first = [
        pltpu.make_async_copy(parent_hbm, parent, sem.at[0]),
        pltpu.make_async_copy(inverse_hbm, inverse, sem.at[1]),
        pltpu.make_async_copy(below_hbm, below, sem.at[2]),
        pltpu.make_async_copy(right_hbm, right, sem.at[3]),
    ]
    quarters = []
    for q in range(4):
        columns = pl.ds((3 - q) * 4 * NB, 4 * NB)
        quarters.append(
            pltpu.make_async_copy(
                coupling_hbm.at[:, columns], coupling.at[:, columns], sem.at[4 + q]
            )
        )
    others = []
    for h in range(1, LEV + 1):
        number = first_number(h) + (leaf >> h)
        others.append(
            pltpu.make_async_copy(sepright_hbm.at[number], sepright.at[h - 1], sem.at[7 + h])
        )
    for copy in first + quarters + others:
        copy.start()
    acc[...] = jnp.zeros_like(acc)
    for copy in first:
        copy.wait()

    factors[LB - 1, :NB, :] = inverse[LB - 1]
    factors[LB - 1, NB:, :] = jnp.zeros((NB, NB), BF16)

    def factor_step(k):
        factors[k, :NB, :] = inverse[k]
        factors[k, NB:, :] = (-mm(below[k], inverse[k])).astype(BF16)

    def forward_step(k):
        result = mm(inverse[k], (right[k] - acc[k]).astype(BF16))
        low = result.astype(BF16)
        rounded[k * NB : (k + 1) * NB, :] = low
        forward_t[k] = result.T.astype(BF16)
        if k < LB - 1:
            p = parent[0, 0, k]
            acc[p] = acc[p] + mm(below[k], low)

    outward = []
    rows = coupling.shape[0] // 2

    def weights_step(k, j):
        own = coupling[j * rows : (j + 1) * rows, k * NB : (k + 1) * NB]
        half = (weights_a, weights_b)[j]
        if k < LB - 1:
            part = jnp.concatenate([own, half[parent[0, 0, k]]], axis=1)
            half[k] = mm(part, factors[k]).astype(BF16)
        else:
            half[k] = mm(own, inverse[k]).astype(BF16)
        target = weights_hbm.at[k, pl.ds(j * rows, rows), :]
        outward.append(pltpu.make_async_copy(half.at[k], target, out_sem.at[2 * k + j]))
        outward[-1].start()

    for k in reversed(range(LB - 1)):
        factor_step(k)
    outward.append(pltpu.make_async_copy(factors, factors_hbm, out_sem.at[2 * LB + 1]))
    outward[-1].start()
    for i in range(LB):
        if i % 4 == 0:
            quarters[i // 4].wait()
        weights_step(LB - 1 - i, 0)
        forward_step(i)
        weights_step(LB - 1 - i, 1)
    outward.append(pltpu.make_async_copy(forward_t, forward_hbm, out_sem.at[2 * LB]))
    outward[-1].start()
    for copy in others:
        copy.wait()
    values = rounded[...]
    first_core = lax.rem(leaf, 2) == 0
    for h in range(1, LEV + 1):
        owner = jnp.logical_and(rep == 0, lax.rem(leaf, 1 << h) == 0)
        flag = jnp.where(owner, 1.0, 0.0).astype(F32)
        for i in range(SB):
            at = (h - 1) * S + i * NB
            block = flag * sepright[h - 1, i * NB : (i + 1) * NB, :] - mm(
                coupling[at : at + NB, :], values
            )
            block = block.T
            upper, lower = block[: NB // 2], block[NB // 2 :]
            keep[:, at : at + NB] = jnp.where(first_core, upper, lower)
            send[:, at : at + NB] = jnp.where(first_core, lower, upper)
    for copy in outward:
        copy.wait()


def triangle(parts, zero):
    rows = (
        jnp.concatenate([parts[0], zero, zero], axis=1),
        jnp.concatenate([parts[1], parts[2], zero], axis=1),
        jnp.concatenate([parts[3], parts[4], parts[5]], axis=1),
    )
    return jnp.concatenate(rows, axis=0)


def separator_kernel(
    place, inverse_hbm, lower_hbm, coupling_hbm, parent_hbm, forward_hbm, factors_hbm,
    base_hbm, full, product,
    blocks, inverse, lowerpart, coupling, parent, forward_t, factors, base, base_low, sem,
):
    shared = first_number(1)
    number = shared + (place[0] >> 1)
    low_rows, low_columns = pl.ds(NB, 2 * NB), pl.ds(0, 2 * NB)
    triangles, couplings = [], []
    for at, size, source in ((0, shared, 0), (shared, 1, number)):
        k = 3 * len(couplings)
        entries = pl.ds(source, size)
        triangles.append(
            pltpu.make_async_copy(inverse_hbm.at[entries], inverse.at[pl.ds(at, size)], sem.at[k])
        )
        triangles.append(
            pltpu.make_async_copy(
                lower_hbm.at[entries, low_rows, low_columns],
                lowerpart.at[pl.ds(at, size)],
                sem.at[k + 1],
            )
        )
        skip = 1 if at == 0 else 0
        couplings.append(
            pltpu.make_async_copy(
                coupling_hbm.at[pl.ds(source - 1 + skip, size - skip)],
                coupling.at[pl.ds(at - 1 + skip, size - skip)],
                sem.at[k + 2],
            )
        )
    fetched = [
        pltpu.make_async_copy(parent_hbm, parent, sem.at[6]),
        pltpu.make_async_copy(forward_hbm, forward_t, sem.at[7]),
        pltpu.make_async_copy(factors_hbm, factors, sem.at[9]),
    ]
    for copy in fetched + triangles + couplings:
        copy.start()
    remaining = list(reversed(range(LB)))

    def base_steps(count):
        for _ in range(min(count, len(remaining))):
            k = remaining.pop(0)
            value = forward_t[k]
            if k < LB - 1:
                value = jnp.concatenate([value, base_low[parent[0, 0, k]]], axis=1)
                value = mm(value, factors[k])
            else:
                value = mm(value, factors[k, :NB, :])
            base[k] = value
            base_low[k] = value.astype(BF16)

    for copy in fetched:
        copy.wait()
    base_steps(3)
    for copy in triangles:
        copy.wait()
    zero = jnp.zeros((NB, NB), BF16)
    one, two, three = slice(0, NB), slice(NB, 2 * NB), slice(2 * NB, 3 * NB)
    members = range(shared + 1)
    inv = {m: [inverse[m, i] for i in range(SB)] for m in members}
    t10 = {m: mm(lowerpart[m, one, one], inv[m][0]).astype(BF16) for m in members}
    base_steps(1)
    t21 = {m: mm(lowerpart[m, two, two], inv[m][1]).astype(BF16) for m in members}
    base_steps(1)
    x10 = {m: (-mm(inv[m][1], t10[m])).astype(BF16) for m in members}
    base_steps(1)
    x21 = {m: (-mm(inv[m][2], t21[m])).astype(BF16) for m in members}
    base_steps(1)
    t20 = {
        m: mm(lowerpart[m, two, :], jnp.concatenate([inv[m][0], x10[m]], axis=0)).astype(BF16)
        for m in members
    }
    base_steps(1)
    x20 = {m: (-mm(inv[m][2], t20[m])).astype(BF16) for m in members}
    for m in members:
        for j, block in enumerate((inv[m][0], x10[m], inv[m][1], x20[m], x21[m], inv[m][2])):
            blocks[m, j] = block
    for h in range(1, LEV + 1):
        full[h - 1] = blocks[shared if h == 1 else first_number(h) + (place[0] >> h)]
    for copy in couplings:
        copy.wait()
    outward = pltpu.make_async_copy(base, base_hbm, sem.at[8])
    for m in members[1:]:
        base_steps(2)
        if m == 4:
            base_steps(LB)
            outward.start()
        matrix = triangle((inv[m][0], x10[m], inv[m][1], x20[m], x21[m], inv[m][2]), zero)
        product[m - 1] = mm(coupling[m - 1], matrix).astype(BF16)
    outward.wait()


def sum_kernel(first, second, out):
    out[...] = first[...] + second[...]


def level_kernel(parts, product, _full, out, residue):
    total = parts[0]
    for j in range(1, parts.shape[0]):
        total = total + parts[j]
    level = total[:, :S]
    residue[...] = level
    second = total[:, S : 2 * S] - mm_nt(level.astype(BF16), product[product.shape[0] - 1])
    for j in range(out.shape[0]):
        out[j, :, :S] = second
        out[j, :, S:] = total[:, 2 * S :]


def tree_kernel(
    place, gathered, residue, full, product, out, res2, res3,
):
    leaf = place[0]
    span = [slice(h * S, (h + 1) * S) for h in range(LEV)]
    residues = []
    for h in range(2, LEV + 1):
        groups = 1 << (LEV - h)
        width = 8 // groups
        children = first_number(h - 1) - 1
        following = []
        for g in range(groups):
            r = gathered[g * width, :, span[h - 2]]
            for j in range(1, width):
                r = r + gathered[g * width + j, :, span[h - 2]]
            if h > 2:
                for c in (2 * g, 2 * g + 1):
                    r = r - mm_nt(residues[c], product[children + c])
            if h == 2:
                res2[g] = r
            if h == 3:
                res3[g] = r
            following.append(r if h == LEV else r.astype(BF16))
        residues = following
    own = [residue[...], res2[leaf >> 2], res3[leaf >> 3], residues[0]]
    scaled = [None] * LEV
    zero = jnp.zeros((NB, NB), BF16)
    for h in range(LEV, 0, -1):
        matrix = triangle([full[h - 1, j] for j in range(6)], zero)
        scaled[h - 1] = mm(mm_nt(own[h - 1].astype(BF16), matrix).astype(BF16), matrix)
    above = None
    for h in range(LEV, 0, -1):
        number = first_number(1) if h == 1 else first_number(h) + (leaf >> h)
        value = scaled[h - 1]
        if h < LEV:
            value = value - mm(above, product[number - 1])
        above = value.astype(BF16)
        for j in range(out.shape[0]):
            out[j, :, span[h - 1]] = value


def finish_kernel(
    place, mine, other, base, weights, local_hbm, separators_hbm, local, separators, out_sem
):
    first_core = lax.rem(place[0], 2) == 0
    a, b = mine[...], other[...]
    rows = jnp.concatenate([jnp.where(first_core, a, b), jnp.where(first_core, b, a)], axis=0)
    low = rows.astype(BF16)
    for i in range(rows.shape[1] // NB):
        separators[i * NB : (i + 1) * NB, :] = rows[:, i * NB : (i + 1) * NB].T
    outward = [pltpu.make_async_copy(separators, separators_hbm, out_sem.at[0])]
    outward[0].start()
    for k in range(0, LB, 2):
        terms = mm(low, jnp.concatenate([weights[k], weights[k + 1]], axis=1))
        for j in range(2):
            value = base[k + j] - terms[:, j * NB : (j + 1) * NB]
            local[(k + j) * NB : (k + j + 1) * NB, :] = value.T
        span = pl.ds(k * NB, 2 * NB)
        outward.append(
            pltpu.make_async_copy(local.at[span], local_hbm.at[span], out_sem.at[1 + k // 2])
        )
        outward[-1].start()
    for copy in outward:
        copy.wait()


def shape(dims, dtype=F32):
    return jax.ShapeDtypeStruct(dims, dtype)


def run_forward(place, parent, right, inverse, below, coupling, separator_right):
    height, rows = coupling.shape
    columns = right.shape[2]
    half = columns // 2
    return pl.pallas_call(
        forward_kernel,
        out_shape=(
            pltpu.HBM((LB, height, NB), BF16),
            pltpu.HBM((LB, columns, NB), BF16),
            pltpu.HBM((LB, 2 * NB, NB), BF16),
            shape((half, height)),
            shape((half, height)),
        ),
        in_specs=[SMEM] + [HBM] * 6,
        out_specs=(HBM,) * 3 + (VMEM,) * 2,
        scratch_shapes=[
            pltpu.VMEM((LB, columns, NB), BF16),
            pltpu.VMEM((LB, 2 * NB, NB), BF16),
            pltpu.VMEM((LB, height // 2, NB), BF16),
            pltpu.VMEM((LB, height // 2, NB), BF16),
            pltpu.SMEM((1, 1, LB - 1), jnp.int32),
            pltpu.VMEM((LB, NB, columns), F32),
            pltpu.VMEM((LB, NB, NB), BF16),
            pltpu.VMEM((LB - 1, NB, NB), BF16),
            pltpu.VMEM((height, rows), BF16),
            pltpu.VMEM((LEV, S, columns), F32),
            pltpu.VMEM((LB, NB, columns), F32),
            pltpu.VMEM((rows, columns), BF16),
            pltpu.SemaphoreType.DMA((12,)),
            pltpu.SemaphoreType.DMA((2 * LB + 2,)),
        ],
        compiler_params=limit(30),
        name="forward",
    )(place, *in_hbm(parent, right, inverse, below, coupling, separator_right))


def run_separator(place, inverse, lowerpart, coupling, parent, forward_t, factors):
    return pl.pallas_call(
        separator_kernel,
        out_shape=(
            pltpu.HBM(forward_t.shape, F32),
            shape((LEV, 6, NB, NB), BF16),
            shape((7, S, S), BF16),
        ),
        in_specs=[SMEM] + [HBM] * 6,
        out_specs=(HBM, VMEM, VMEM),
        scratch_shapes=[
            pltpu.VMEM((8, 6, NB, NB), BF16),
            pltpu.VMEM((8, SB, NB, NB), BF16),
            pltpu.VMEM((8, 2 * NB, 2 * NB), BF16),
            pltpu.VMEM((7, S, S), BF16),
            pltpu.SMEM((1, 1, LB - 1), jnp.int32),
            pltpu.VMEM(forward_t.shape, BF16),
            pltpu.VMEM(factors.shape, BF16),
            pltpu.VMEM(forward_t.shape, F32),
            pltpu.VMEM(forward_t.shape, BF16),
            pltpu.SemaphoreType.DMA((10,)),
        ],
        compiler_params=limit(16),
        cost_estimate=pl.CostEstimate(flops=6 * 10**9, transcendentals=0, bytes_accessed=2 * 10**7),
        name="separator",
    )(place, *in_hbm(inverse, lowerpart, coupling, parent, forward_t, factors))


def on_device(
    local_right,
    local_inverse,
    local_below,
    local_parent,
    local_coupling,
    separator_right,
    separator_inverse,
    separator_lower,
    parent_coupling,
):
    rows = local_right.shape[2]
    columns = local_right.shape[3]
    half = columns // 2
    height = LEV * S
    leaves = lax.axis_size("leaf")
    reps = lax.axis_size("rep")
    chips = [[2 * i + c for i in range(leaves // 2)] for c in range(2)]
    pairs = [(i, i ^ 1) for i in range(leaves)]
    place = jnp.stack([lax.axis_index("leaf"), lax.axis_index("rep")]).astype(jnp.int32)
    right = local_right.reshape(LB, NB, columns)
    coupling = local_coupling.reshape(height, rows)

    weights, forward_t, factors, keep, send = run_forward(
        place, local_parent, right, local_inverse[0, 0], local_below[0, 0], coupling, separator_right
    )
    total = pl.pallas_call(
        sum_kernel,
        out_shape=shape((half, height)),
        in_specs=[VMEM] * 2,
        out_specs=VMEM,
        compiler_params=limit(8),
        name="sum",
    )(keep, lax.ppermute(send, "leaf", pairs))
    parts = lax.all_to_all(total.reshape(reps, CH, height), "rep", 0, 0, tiled=True)
    place_after, _ = lax.optimization_barrier((place, total))
    base, full, product = run_separator(
        place_after, separator_inverse, separator_lower, parent_coupling, local_parent, forward_t, factors
    )
    parts, full, base, product = lax.optimization_barrier((parts, full, base, product))
    summed, residue = pl.pallas_call(
        level_kernel,
        out_shape=(shape((leaves // 2, CH, height - S)), shape((CH, S))),
        in_specs=[VMEM] * 2 + [pl.BlockSpec(memory_space=pl.ANY)],
        out_specs=(VMEM, VMEM),
        compiler_params=limit(8),
        name="level",
    )(parts, product, full)
    gathered = lax.all_to_all(summed, "leaf", 0, 0, axis_index_groups=chips, tiled=True)
    solved = pl.pallas_call(
        tree_kernel,
        out_shape=shape((reps, CH, height)),
        in_specs=[SMEM] + [VMEM] * 4,
        out_specs=VMEM,
        scratch_shapes=[
            pltpu.VMEM((4, CH, S), F32),
            pltpu.VMEM((2, CH, S), F32),
        ],
        compiler_params=limit(12),
        cost_estimate=pl.CostEstimate(flops=6 * 10**9, transcendentals=0, bytes_accessed=4 * 10**7),
        name="tree",
    )(place, gathered, residue, full, product)
    mine = lax.all_to_all(solved, "rep", 0, 0, tiled=True).reshape(half, height)
    other = lax.ppermute(mine, "leaf", pairs)
    local, separators = pl.pallas_call(
        finish_kernel,
        out_shape=(pltpu.HBM((rows, columns), F32), pltpu.HBM((height, columns), F32)),
        in_specs=[SMEM] + [VMEM] * 4,
        out_specs=(HBM, HBM),
        scratch_shapes=[
            pltpu.VMEM((rows, columns), F32),
            pltpu.VMEM((height, columns), F32),
            pltpu.SemaphoreType.DMA((LB // 2 + 1,)),
        ],
        compiler_params=limit(16),
        name="finish",
    )(place, mine, other, base, weights)
    return (local[None, None], separators.reshape(1, LEV, S, columns))


def solution(mesh):
    in_specs = (
        P("leaf", "rep", None, None),
        P("leaf", "rep", None, None, None),
        P("leaf", "rep", None, None, None),
        P("leaf", "rep", None),
        P("leaf", "rep", None, None, None),
        P(),
        P(),
        P(),
        P(),
    )
    out_specs = (P("leaf", "rep", None, None), P("leaf", None, None, None))
    return jax.shard_map(
        on_device, mesh=mesh, in_specs=in_specs, out_specs=out_specs, check_vma=False
    )
```

```python
import jax
import jax.numpy as jnp
from jax import lax
from jax.experimental import pallas as pl
from jax.experimental.pallas import tpu as pltpu
from jax.sharding import PartitionSpec as P

NB = 128
LB = 16
SB = 3
S = SB * NB
LEV = 4
CH = 8
F32 = jnp.float32
BF16 = jnp.bfloat16
VMEM = pl.BlockSpec(memory_space=pltpu.VMEM)
SMEM = pl.BlockSpec(memory_space=pltpu.SMEM)
HBM = pl.BlockSpec(memory_space=pltpu.HBM)


def in_hbm(*arrays):
    return [pltpu.with_memory_space_constraint(array, pltpu.HBM) for array in arrays]


def limit(mib):
    return pltpu.CompilerParams(vmem_limit_bytes=mib << 20)


def mm(a, b):
    return jnp.dot(a, b, preferred_element_type=F32)


def mm_nt(a, b):
    return lax.dot_general(a, b, (((1,), (1,)), ((), ())), preferred_element_type=F32)


def first_number(height):
    return (1 << (LEV - height)) - 1


def forward_kernel(
    place, parent_hbm, right_hbm, inverse_hbm, below_hbm, coupling_hbm, sepright_hbm,
    weights_hbm, forward_hbm, factors_hbm, keep, send,
    forward_t, factors, weights_a, weights_b,
    parent, right, inverse, below, coupling, sepright, acc, rounded, sem, out_sem,
):
    leaf, rep = place[0], place[1]
    first = [
        pltpu.make_async_copy(parent_hbm, parent, sem.at[0]),
        pltpu.make_async_copy(inverse_hbm, inverse, sem.at[1]),
        pltpu.make_async_copy(below_hbm, below, sem.at[2]),
        pltpu.make_async_copy(right_hbm, right, sem.at[3]),
    ]
    quarters = []
    for q in range(4):
        columns = pl.ds((3 - q) * 4 * NB, 4 * NB)
        quarters.append(
            pltpu.make_async_copy(
                coupling_hbm.at[:, columns], coupling.at[:, columns], sem.at[4 + q]
            )
        )
    others = []
    for h in range(1, LEV + 1):
        number = first_number(h) + (leaf >> h)
        others.append(
            pltpu.make_async_copy(sepright_hbm.at[number], sepright.at[h - 1], sem.at[7 + h])
        )
    for copy in first + quarters + others:
        copy.start()
    acc[...] = jnp.zeros_like(acc)
    for copy in first:
        copy.wait()

    factors[LB - 1, :NB, :] = inverse[LB - 1]
    factors[LB - 1, NB:, :] = jnp.zeros((NB, NB), BF16)

    def factor_step(k):
        factors[k, :NB, :] = inverse[k]
        factors[k, NB:, :] = (-mm(below[k], inverse[k])).astype(BF16)

    def forward_step(k):
        result = mm(inverse[k], (right[k] - acc[k]).astype(BF16))
        low = result.astype(BF16)
        rounded[k * NB : (k + 1) * NB, :] = low
        forward_t[k] = result.T.astype(BF16)
        if k < LB - 1:
            p = parent[0, 0, k]
            acc[p] = acc[p] + mm(below[k], low)

    outward = []
    rows = coupling.shape[0] // 2

    def weights_step(k, j):
        own = coupling[j * rows : (j + 1) * rows, k * NB : (k + 1) * NB]
        half = (weights_a, weights_b)[j]
        if k < LB - 1:
            part = jnp.concatenate([own, half[parent[0, 0, k]]], axis=1)
            half[k] = mm(part, factors[k]).astype(BF16)
        else:
            half[k] = mm(own, inverse[k]).astype(BF16)
        target = weights_hbm.at[k, pl.ds(j * rows, rows), :]
        outward.append(pltpu.make_async_copy(half.at[k], target, out_sem.at[2 * k + j]))
        outward[-1].start()

    for k in reversed(range(LB - 1)):
        factor_step(k)
    outward.append(pltpu.make_async_copy(factors, factors_hbm, out_sem.at[2 * LB + 1]))
    outward[-1].start()
    for i in range(LB):
        if i % 4 == 0:
            quarters[i // 4].wait()
        weights_step(LB - 1 - i, 0)
        forward_step(i)
        weights_step(LB - 1 - i, 1)
    outward.append(pltpu.make_async_copy(forward_t, forward_hbm, out_sem.at[2 * LB]))
    outward[-1].start()
    for copy in others:
        copy.wait()
    values = rounded[...]
    first_core = lax.rem(leaf, 2) == 0
    for h in range(1, LEV + 1):
        owner = jnp.logical_and(rep == 0, lax.rem(leaf, 1 << h) == 0)
        flag = jnp.where(owner, 1.0, 0.0).astype(F32)
        for i in range(SB):
            at = (h - 1) * S + i * NB
            block = flag * sepright[h - 1, i * NB : (i + 1) * NB, :] - mm(
                coupling[at : at + NB, :], values
            )
            block = block.T
            upper, lower = block[: NB // 2], block[NB // 2 :]
            keep[:, at : at + NB] = jnp.where(first_core, upper, lower)
            send[:, at : at + NB] = jnp.where(first_core, lower, upper)
    for copy in outward:
        copy.wait()


def triangle(parts, zero):
    rows = (
        jnp.concatenate([parts[0], zero, zero], axis=1),
        jnp.concatenate([parts[1], parts[2], zero], axis=1),
        jnp.concatenate([parts[3], parts[4], parts[5]], axis=1),
    )
    return jnp.concatenate(rows, axis=0)


def separator_kernel(
    place, inverse_hbm, lower_hbm, coupling_hbm, parent_hbm, forward_hbm, factors_hbm,
    base_hbm, full, product,
    blocks, inverse, lowerpart, coupling, parent, forward_t, factors, base, base_low, sem,
):
    shared = first_number(1)
    number = shared + (place[0] >> 1)
    low_rows, low_columns = pl.ds(NB, 2 * NB), pl.ds(0, 2 * NB)
    triangles, couplings = [], []
    for at, size, source in ((0, shared, 0), (shared, 1, number)):
        k = 3 * len(couplings)
        entries = pl.ds(source, size)
        triangles.append(
            pltpu.make_async_copy(inverse_hbm.at[entries], inverse.at[pl.ds(at, size)], sem.at[k])
        )
        triangles.append(
            pltpu.make_async_copy(
                lower_hbm.at[entries, low_rows, low_columns],
                lowerpart.at[pl.ds(at, size)],
                sem.at[k + 1],
            )
        )
        skip = 1 if at == 0 else 0
        couplings.append(
            pltpu.make_async_copy(
                coupling_hbm.at[pl.ds(source - 1 + skip, size - skip)],
                coupling.at[pl.ds(at - 1 + skip, size - skip)],
                sem.at[k + 2],
            )
        )
    fetched = [
        pltpu.make_async_copy(parent_hbm, parent, sem.at[6]),
        pltpu.make_async_copy(forward_hbm, forward_t, sem.at[7]),
        pltpu.make_async_copy(factors_hbm, factors, sem.at[9]),
    ]
    for copy in fetched + triangles + couplings:
        copy.start()
    remaining = list(reversed(range(LB)))

    def base_steps(count):
        for _ in range(min(count, len(remaining))):
            k = remaining.pop(0)
            value = forward_t[k]
            if k < LB - 1:
                value = jnp.concatenate([value, base_low[parent[0, 0, k]]], axis=1)
                value = mm(value, factors[k])
            else:
                value = mm(value, factors[k, :NB, :])
            base[k] = value
            base_low[k] = value.astype(BF16)

    for copy in fetched:
        copy.wait()
    base_steps(3)
    for copy in triangles:
        copy.wait()
    zero = jnp.zeros((NB, NB), BF16)
    one, two, three = slice(0, NB), slice(NB, 2 * NB), slice(2 * NB, 3 * NB)
    members = range(shared + 1)
    inv = {m: [inverse[m, i] for i in range(SB)] for m in members}
    t10 = {m: mm(lowerpart[m, one, one], inv[m][0]).astype(BF16) for m in members}
    base_steps(1)
    t21 = {m: mm(lowerpart[m, two, two], inv[m][1]).astype(BF16) for m in members}
    base_steps(1)
    x10 = {m: (-mm(inv[m][1], t10[m])).astype(BF16) for m in members}
    base_steps(1)
    x21 = {m: (-mm(inv[m][2], t21[m])).astype(BF16) for m in members}
    base_steps(1)
    t20 = {
        m: mm(lowerpart[m, two, :], jnp.concatenate([inv[m][0], x10[m]], axis=0)).astype(BF16)
        for m in members
    }
    base_steps(1)
    x20 = {m: (-mm(inv[m][2], t20[m])).astype(BF16) for m in members}
    for m in members:
        for j, block in enumerate((inv[m][0], x10[m], inv[m][1], x20[m], x21[m], inv[m][2])):
            blocks[m, j] = block
    for h in range(1, LEV + 1):
        full[h - 1] = blocks[shared if h == 1 else first_number(h) + (place[0] >> h)]
    for copy in couplings:
        copy.wait()
    outward = pltpu.make_async_copy(base, base_hbm, sem.at[8])
    for m in members[1:]:
        base_steps(2)
        if m == 4:
            base_steps(LB)
            outward.start()
        matrix = triangle((inv[m][0], x10[m], inv[m][1], x20[m], x21[m], inv[m][2]), zero)
        product[m - 1] = mm(coupling[m - 1], matrix).astype(BF16)
    outward.wait()


def sum_kernel(first, second, out):
    out[...] = first[...] + second[...]


def level_kernel(parts, product, _full, out, residue):
    total = parts[0]
    for j in range(1, parts.shape[0]):
        total = total + parts[j]
    level = total[:, :S]
    residue[...] = level
    second = total[:, S : 2 * S] - mm_nt(level.astype(BF16), product[product.shape[0] - 1])
    for j in range(out.shape[0]):
        out[j, :, :S] = second
        out[j, :, S:] = total[:, 2 * S :]


def tree_kernel(
    place, gathered, residue, full, product, out, res2, res3,
):
    leaf = place[0]
    span = [slice(h * S, (h + 1) * S) for h in range(LEV)]
    residues = []
    for h in range(2, LEV + 1):
        groups = 1 << (LEV - h)
        width = 8 // groups
        children = first_number(h - 1) - 1
        following = []
        for g in range(groups):
            r = gathered[g * width, :, span[h - 2]]
            for j in range(1, width):
                r = r + gathered[g * width + j, :, span[h - 2]]
            if h > 2:
                for c in (2 * g, 2 * g + 1):
                    r = r - mm_nt(residues[c], product[children + c])
            if h == 2:
                res2[g] = r
            if h == 3:
                res3[g] = r
            following.append(r if h == LEV else r.astype(BF16))
        residues = following
    own = [residue[...], res2[leaf >> 2], res3[leaf >> 3], residues[0]]
    scaled = [None] * LEV
    zero = jnp.zeros((NB, NB), BF16)
    for h in range(LEV, 0, -1):
        matrix = triangle([full[h - 1, j] for j in range(6)], zero)
        scaled[h - 1] = mm(mm_nt(own[h - 1].astype(BF16), matrix).astype(BF16), matrix)
    above = None
    for h in range(LEV, 0, -1):
        number = first_number(1) if h == 1 else first_number(h) + (leaf >> h)
        value = scaled[h - 1]
        if h < LEV:
            value = value - mm(above, product[number - 1])
        above = value.astype(BF16)
        for j in range(out.shape[0]):
            out[j, :, span[h - 1]] = value


def finish_kernel(
    place, mine, other, base, weights, local_hbm, separators_hbm, local, separators, out_sem
):
    first_core = lax.rem(place[0], 2) == 0
    a, b = mine[...], other[...]
    rows = jnp.concatenate([jnp.where(first_core, a, b), jnp.where(first_core, b, a)], axis=0)
    low = rows.astype(BF16)
    outward = [pltpu.make_async_copy(separators, separators_hbm, out_sem.at[0])]
    for k in range(0, LB, 2):
        terms = mm(low, jnp.concatenate([weights[k], weights[k + 1]], axis=1))
        for i in range(2 * k, min(2 * k + 4, rows.shape[1] // NB)):
            separators[i * NB : (i + 1) * NB, :] = rows[:, i * NB : (i + 1) * NB].T
        if k == 4:
            outward[0].start()
        for j in range(2):
            value = base[k + j] - terms[:, j * NB : (j + 1) * NB]
            local[(k + j) * NB : (k + j + 1) * NB, :] = value.T
        span = pl.ds(k * NB, 2 * NB)
        outward.append(
            pltpu.make_async_copy(local.at[span], local_hbm.at[span], out_sem.at[1 + k // 2])
        )
        outward[-1].start()
    for copy in outward:
        copy.wait()


def shape(dims, dtype=F32):
    return jax.ShapeDtypeStruct(dims, dtype)


def run_forward(place, parent, right, inverse, below, coupling, separator_right):
    height, rows = coupling.shape
    columns = right.shape[2]
    half = columns // 2
    return pl.pallas_call(
        forward_kernel,
        out_shape=(
            pltpu.HBM((LB, height, NB), BF16),
            pltpu.HBM((LB, columns, NB), BF16),
            pltpu.HBM((LB, 2 * NB, NB), BF16),
            shape((half, height)),
            shape((half, height)),
        ),
        in_specs=[SMEM] + [HBM] * 6,
        out_specs=(HBM,) * 3 + (VMEM,) * 2,
        scratch_shapes=[
            pltpu.VMEM((LB, columns, NB), BF16),
            pltpu.VMEM((LB, 2 * NB, NB), BF16),
            pltpu.VMEM((LB, height // 2, NB), BF16),
            pltpu.VMEM((LB, height // 2, NB), BF16),
            pltpu.SMEM((1, 1, LB - 1), jnp.int32),
            pltpu.VMEM((LB, NB, columns), F32),
            pltpu.VMEM((LB, NB, NB), BF16),
            pltpu.VMEM((LB - 1, NB, NB), BF16),
            pltpu.VMEM((height, rows), BF16),
            pltpu.VMEM((LEV, S, columns), F32),
            pltpu.VMEM((LB, NB, columns), F32),
            pltpu.VMEM((rows, columns), BF16),
            pltpu.SemaphoreType.DMA((12,)),
            pltpu.SemaphoreType.DMA((2 * LB + 2,)),
        ],
        compiler_params=limit(30),
        name="forward",
    )(place, *in_hbm(parent, right, inverse, below, coupling, separator_right))


def run_separator(place, inverse, lowerpart, coupling, parent, forward_t, factors):
    return pl.pallas_call(
        separator_kernel,
        out_shape=(
            pltpu.HBM(forward_t.shape, F32),
            shape((LEV, 6, NB, NB), BF16),
            shape((7, S, S), BF16),
        ),
        in_specs=[SMEM] + [HBM] * 6,
        out_specs=(HBM, VMEM, VMEM),
        scratch_shapes=[
            pltpu.VMEM((8, 6, NB, NB), BF16),
            pltpu.VMEM((8, SB, NB, NB), BF16),
            pltpu.VMEM((8, 2 * NB, 2 * NB), BF16),
            pltpu.VMEM((7, S, S), BF16),
            pltpu.SMEM((1, 1, LB - 1), jnp.int32),
            pltpu.VMEM(forward_t.shape, BF16),
            pltpu.VMEM(factors.shape, BF16),
            pltpu.VMEM(forward_t.shape, F32),
            pltpu.VMEM(forward_t.shape, BF16),
            pltpu.SemaphoreType.DMA((10,)),
        ],
        compiler_params=limit(16),
        cost_estimate=pl.CostEstimate(flops=6 * 10**9, transcendentals=0, bytes_accessed=2 * 10**7),
        name="separator",
    )(place, *in_hbm(inverse, lowerpart, coupling, parent, forward_t, factors))


def on_device(
    local_right,
    local_inverse,
    local_below,
    local_parent,
    local_coupling,
    separator_right,
    separator_inverse,
    separator_lower,
    parent_coupling,
):
    rows = local_right.shape[2]
    columns = local_right.shape[3]
    half = columns // 2
    height = LEV * S
    leaves = lax.axis_size("leaf")
    reps = lax.axis_size("rep")
    chips = [[2 * i + c for i in range(leaves // 2)] for c in range(2)]
    pairs = [(i, i ^ 1) for i in range(leaves)]
    place = jnp.stack([lax.axis_index("leaf"), lax.axis_index("rep")]).astype(jnp.int32)
    right = local_right.reshape(LB, NB, columns)
    coupling = local_coupling.reshape(height, rows)

    weights, forward_t, factors, keep, send = run_forward(
        place, local_parent, right, local_inverse[0, 0], local_below[0, 0], coupling, separator_right
    )
    total = pl.pallas_call(
        sum_kernel,
        out_shape=shape((half, height)),
        in_specs=[VMEM] * 2,
        out_specs=VMEM,
        compiler_params=limit(8),
        name="sum",
    )(keep, lax.ppermute(send, "leaf", pairs))
    parts = lax.all_to_all(total.reshape(reps, CH, height), "rep", 0, 0, tiled=True)
    place_after, _ = lax.optimization_barrier((place, total))
    base, full, product = run_separator(
        place_after, separator_inverse, separator_lower, parent_coupling, local_parent, forward_t, factors
    )
    parts, full, base, product = lax.optimization_barrier((parts, full, base, product))
    summed, residue = pl.pallas_call(
        level_kernel,
        out_shape=(shape((leaves // 2, CH, height - S)), shape((CH, S))),
        in_specs=[VMEM] * 2 + [pl.BlockSpec(memory_space=pl.ANY)],
        out_specs=(VMEM, VMEM),
        compiler_params=limit(8),
        name="level",
    )(parts, product, full)
    gathered = lax.all_to_all(summed, "leaf", 0, 0, axis_index_groups=chips, tiled=True)
    solved = pl.pallas_call(
        tree_kernel,
        out_shape=shape((reps, CH, height)),
        in_specs=[SMEM] + [VMEM] * 4,
        out_specs=VMEM,
        scratch_shapes=[
            pltpu.VMEM((4, CH, S), F32),
            pltpu.VMEM((2, CH, S), F32),
        ],
        compiler_params=limit(12),
        cost_estimate=pl.CostEstimate(flops=6 * 10**9, transcendentals=0, bytes_accessed=4 * 10**7),
        name="tree",
    )(place, gathered, residue, full, product)
    mine = lax.all_to_all(solved, "rep", 0, 0, tiled=True).reshape(half, height)
    other = lax.ppermute(mine, "leaf", pairs)
    local, separators = pl.pallas_call(
        finish_kernel,
        out_shape=(pltpu.HBM((rows, columns), F32), pltpu.HBM((height, columns), F32)),
        in_specs=[SMEM] + [VMEM] * 4,
        out_specs=(HBM, HBM),
        scratch_shapes=[
            pltpu.VMEM((rows, columns), F32),
            pltpu.VMEM((height, columns), F32),
            pltpu.SemaphoreType.DMA((LB // 2 + 1,)),
        ],
        compiler_params=limit(16),
        name="finish",
    )(place, mine, other, base, weights)
    return (local[None, None], separators.reshape(1, LEV, S, columns))


def solution(mesh):
    in_specs = (
        P("leaf", "rep", None, None),
        P("leaf", "rep", None, None, None),
        P("leaf", "rep", None, None, None),
        P("leaf", "rep", None),
        P("leaf", "rep", None, None, None),
        P(),
        P(),
        P(),
        P(),
    )
    out_specs = (P("leaf", "rep", None, None), P("leaf", None, None, None))
    return jax.shard_map(
        on_device, mesh=mesh, in_specs=in_specs, out_specs=out_specs, check_vma=False
    )
```
